768 devices in a mesh: seq: 96 (over y, z), head: 8 (over x, core).
Axes of the slice: x: 4, y: 8, z: 12, core: 2. Of those that a mesh axis runs over, the one named last changes fastest.
Arguments:
- queries: bfloat16 [24576, 8192], P('seq', 'head'), may hold values from -125 to 125
- keys: bfloat16 [24576, 1024], P(('seq', 'head')), may hold values from -6 to 6
- values: bfloat16 [24576, 1024], P(('seq', 'head')), may hold values from -6 to 6
- header: int32 [192], P('seq'), may hold values from 0 to 191, as said below
- related: int32 [192, 3], P('seq'), may hold values from 0 to 191, as said below
- upstream: bfloat16 [24576, 8192], P('seq', 'head'), may hold values from -6 to 6
Outputs:
- attended: bfloat16 [24576, 8192], P('seq', 'head')
- query_grad: bfloat16 [24576, 8192], P('seq', 'head')
- key_grad: float32 [24576, 1024], P(('seq', 'head'))
- value_grad: float32 [24576, 1024], P(('seq', 'head'))
The draws below stay inside these ranges and needn't reach their ends.
Inputs may be any that keep to these rules, and one draw needn't show every extreme that they name: Tables are runs of 1 to 8 consecutive row blocks, one of exactly 8, and the last row block is a table of its own; header[b] is the first block of the table that holds b. related[b, r] lies between header[b] and b.
All inputs are finite; a program needn't handle non-finite values.
Results may differ from the reference program's by a relative error of at most 0.04.
Values may be sent and summed in bfloat16 or wider, within the bound.
A program may use at most 32 MiB of HBM per device.

```python
import math
import jax
import jax.numpy as jnp
from jax import lax

BLOCK = 128
HEAD_DIM = 128
GROUP = 8
TABLE_MAX = 8
KV_HEADS = 8
HEADS = 64
NBLOCKS = 192
TOKENS = 24576


def table_layout(key):
    length_key = jax.random.fold_in(key, 11)
    lengths = jax.random.randint(length_key, (NBLOCKS,), 1, TABLE_MAX + 1).astype(jnp.int32)
    lengths = lengths.at[0].set(TABLE_MAX)
    starts = jnp.cumsum(lengths) - lengths
    block_ids = jnp.arange(NBLOCKS, dtype=jnp.int32)
    candidate = jnp.where(starts[None, :] <= block_ids[:, None], starts[None, :], 0)
    header = jnp.max(candidate, axis=1).astype(jnp.int32)
    header = jnp.where(block_ids == NBLOCKS - 1, NBLOCKS - 1, header).astype(jnp.int32)
    pick_key = jax.random.fold_in(key, 12)
    picks = jax.random.randint(pick_key, (NBLOCKS, 3), 0, 1 << 20).astype(jnp.int32)
    extent = block_ids - header + 1
    related = (header[:, None] + picks % extent[:, None]).astype(jnp.int32)
    return (header, related)


def draw_header(key, part):
    return table_layout(key)[0]


def draw_related(key, part):
    return table_layout(key)[1]


def drawn_pair(key):
    base_keys = jnp.clip(jax.random.normal(jax.random.fold_in(key, 21), (TOKENS, KV_HEADS * HEAD_DIM), jnp.float32), -5.0, 5.0)
    base_queries = jnp.clip(jax.random.normal(jax.random.fold_in(key, 22), (TOKENS, HEADS * HEAD_DIM), jnp.float32), -5.0, 5.0)
    final_keys = base_keys
    final_queries = base_queries
    return (final_queries, final_keys)


def draw_queries(key, part):
    return drawn_pair(key)[0].astype(jnp.bfloat16)


def draw_keys(key, part):
    return drawn_pair(key)[1].astype(jnp.bfloat16)


def block_scale(stream_key, shape, shards, low, top_value):
    def one(dim, parts):
        steps = jax.random.uniform(jax.random.fold_in(jax.random.fold_in(stream_key, 6), dim), (parts,), jnp.float32, low / len(shards), top_value / len(shards))
        return jnp.repeat(jnp.exp(steps), shape[dim] // parts).reshape((-1,) + (1,) * (len(shape) - dim - 1))

    level = one(*shards[0])
    for cut in shards[1:]:
        level = level * one(*cut)
    return level


def noise(stream_key, shape, scale, reach, cuts=(), kind=jnp.bfloat16):
    entries = jax.random.normal(stream_key, shape, jnp.float32) * scale
    if len(cuts) > 0:
        entries = block_scale(stream_key, shape, cuts, -0.22, 0.18) * entries
    return jnp.clip(entries, min=-reach, max=reach).astype(kind)


def setup_inputs(seed: int = 0) -> dict:
    streams_of = jax.random.split(jax.random.key(seed), 7)
    return {
        "queries": draw_queries(jax.random.fold_in(streams_of[6], 71), 0),
        "keys": draw_keys(jax.random.fold_in(streams_of[6], 71), 0),
        "values": noise(streams_of[2], (TOKENS, KV_HEADS * HEAD_DIM), 1.0, 6.0, ((0, 768),)),
        "header": draw_header(jax.random.fold_in(streams_of[6], 71), 0),
        "related": draw_related(jax.random.fold_in(streams_of[6], 71), 0),
        "upstream": noise(streams_of[5], (TOKENS, HEADS * HEAD_DIM), 1.0, 6.0, ((0, 96), (1, 8))),
    }


def reference(queries, keys, values, header, related, upstream):
    score_scale = 1.0 / math.sqrt(HEAD_DIM)
    block_ids = jnp.arange(NBLOCKS, dtype=jnp.int32)
    listed = jnp.stack([block_ids, (block_ids - 1) % NBLOCKS, header, related[:, 0], related[:, 1], related[:, 2]], axis=1).astype(jnp.int32)
    query_blocks = queries.reshape(NBLOCKS, BLOCK, KV_HEADS, GROUP, HEAD_DIM)
    upstream_blocks = upstream.reshape(NBLOCKS, BLOCK, KV_HEADS, GROUP, HEAD_DIM)
    key_blocks = keys.reshape(NBLOCKS, BLOCK, KV_HEADS, HEAD_DIM)
    value_blocks = values.reshape(NBLOCKS, BLOCK, KV_HEADS, HEAD_DIM)

    def one_block(accumulators, inputs):
        key_acc, value_acc = accumulators
        query_blk, upstream_blk, slot_ids = inputs
        key_rows = key_blocks[slot_ids].reshape(6 * BLOCK, KV_HEADS, HEAD_DIM).astype(jnp.float32)
        value_rows = value_blocks[slot_ids].reshape(6 * BLOCK, KV_HEADS, HEAD_DIM).astype(jnp.float32)
        query_wide = query_blk.astype(jnp.float32)
        upstream_wide = upstream_blk.astype(jnp.float32)
        scores = jnp.einsum('igjd,cgd->gjic', query_wide, key_rows) * score_scale
        top_score = lax.optimization_barrier(jnp.max(scores, axis=-1, keepdims=True))
        weights_exp = jnp.exp(scores - top_score)
        probs = weights_exp / lax.optimization_barrier(jnp.sum(weights_exp, axis=-1, keepdims=True))
        probs_low = probs.astype(jnp.bfloat16).astype(jnp.float32)
        attended = jnp.einsum('gjic,cgd->igjd', probs_low, value_rows).astype(jnp.bfloat16)
        delta = jnp.einsum('igjd,igjd->gji', upstream_wide, attended.astype(jnp.float32))
        dprobs = jnp.einsum('igjd,cgd->gjic', upstream_wide, value_rows)
        dscores = probs * (dprobs - delta[..., None])
        dscores_low = dscores.astype(jnp.bfloat16).astype(jnp.float32)
        query_grad = (jnp.einsum('gjic,cgd->igjd', dscores_low, key_rows) * score_scale).astype(jnp.bfloat16)
        key_part = jnp.einsum('gjic,igjd->cgd', dscores_low, query_wide) * score_scale
        value_part = jnp.einsum('gjic,igjd->cgd', probs_low, upstream_wide)
        key_acc = key_acc.at[slot_ids].add(key_part.reshape(6, BLOCK, KV_HEADS, HEAD_DIM))
        value_acc = value_acc.at[slot_ids].add(value_part.reshape(6, BLOCK, KV_HEADS, HEAD_DIM))
        return ((key_acc, value_acc), (attended, query_grad))
    start_acc = jnp.zeros((NBLOCKS, BLOCK, KV_HEADS, HEAD_DIM), jnp.float32)
    (key_acc, value_acc), (attended, query_grad) = lax.scan(one_block, (start_acc, start_acc), (query_blocks, upstream_blocks, listed))
    attended = attended.reshape(TOKENS, HEADS * HEAD_DIM)
    query_grad = query_grad.reshape(TOKENS, HEADS * HEAD_DIM)
    key_grad = key_acc.reshape(TOKENS, KV_HEADS * HEAD_DIM)
    value_grad = value_acc.reshape(TOKENS, KV_HEADS * HEAD_DIM)
    return (attended, query_grad, key_grad, value_grad)
```

```python
import functools
import math

import jax
import jax.numpy as jnp
from jax import lax
from jax.experimental import pallas as pl
from jax.experimental.pallas import tpu as pltpu
from jax.sharding import PartitionSpec as P

BLOCK = 128
D = 128
GROUP = 8
QROWS = BLOCK * GROUP
SPAN = 8
NPOS = 9
REACH = 4
QT = 512
BIG = 1e30
SCALE = 1.0 / math.sqrt(D)
C2 = SCALE * math.log2(math.e)
LOG2 = [math.log2(n) if n else 0.0 for n in range(SPAN)]
NT = (((1,), (1,)), ((), ()))
NN = (((1,), (0,)), ((), ()))
F32 = jnp.float32
BF16 = jnp.bfloat16


def dot(a, b, dims=NN):
    return lax.dot_general(a, b, dims, preferred_element_type=F32)


def kernel(
    seq_n,
    head_n,
    header,
    related,
    q_hbm,
    u_hbm,
    k_hbm,
    v_hbm,
    att_hbm,
    dq_hbm,
    dk_hbm,
    dv_hbm,
    q_r,
    u_r,
    win,
    tr,
    pbuf,
    dpbuf,
    plow,
    dlow,
    stats,
    mhist,
    sbuf,
    rbuf,
    gbuf,
    backb,
    widen,
    final,
    att_v,
    dq_v,
    a_send,
    a_recv,
    f_send,
    f_recv,
    r_send,
    r_recv,
    b_send,
    b_recv,
    ld_sem,
    out_sem,
):
    seq = lax.axis_index("seq")
    me = lax.axis_index("head")
    nxt = lax.rem(seq + 1, seq_n)
    prv = lax.rem(seq + seq_n - 1, seq_n)
    part = (2 * BLOCK) // head_n
    half = head_n // 2
    own = (NPOS - 2) * BLOCK

    barrier = pltpu.get_barrier_semaphore()
    for off in range(1, head_n):
        pl.semaphore_signal(
            barrier, inc=1, device_id={"head": lax.rem(me + off, head_n)}
        )
    pl.semaphore_signal(barrier, inc=1, device_id={"seq": nxt})
    pl.semaphore_signal(barrier, inc=1, device_id={"seq": prv})

    def load(n):
        t, j = n // GROUP, n % GROUP
        rows, cols = pl.ds(t * BLOCK, BLOCK), pl.ds(j * D, D)
        at = pl.ds(n * BLOCK, BLOCK)
        return (
            pltpu.make_async_copy(q_hbm.at[rows, cols], q_r.at[at, :], ld_sem.at[0, n]),
            pltpu.make_async_copy(u_hbm.at[rows, cols], u_r.at[at, :], ld_sem.at[1, n]),
        )

    for n in range(2 * GROUP):
        for copy in load(n):
            copy.start()

    pl.semaphore_wait(barrier, head_n + 1)

    def mine(x, h):
        return pl.ds(own + h * part, part)

    sends = []
    for x, src in ((0, k_hbm), (1, v_hbm)):
        pltpu.make_async_copy(
            src.at[:, pl.ds(me * D, D)],
            win.at[x, pl.ds(own + me * part, part), :],
            a_recv.at[x, me],
        ).start()
        for off in range(1, head_n):
            peer = lax.rem(me + off, head_n)
            copy = pltpu.make_async_remote_copy(
                src_ref=src.at[:, pl.ds(peer * D, D)],
                dst_ref=win.at[x, pl.ds(own + me * part, part), :],
                send_sem=a_send.at[x, off],
                recv_sem=a_recv.at[x, me],
                device_id={"head": peer},
            )
            copy.start()
            sends.append(copy)

    def gathered(x, hi):
        for h in range(half * hi, half * hi + half):
            ref = win.at[x, pl.ds(own + h * part, part), :]
            pltpu.make_async_copy(ref, ref, a_recv.at[x, h]).wait()

    def forward(x, k, hi):
        at = (NPOS - 2 - 2 * k + hi) * BLOCK
        return pltpu.make_async_remote_copy(
            src_ref=win.at[x, pl.ds(at, BLOCK), :],
            dst_ref=win.at[x, pl.ds(at - 2 * BLOCK, BLOCK), :],
            send_sem=f_send.at[x, k, hi],
            recv_sem=f_recv.at[x, k, hi],
            device_id={"seq": nxt},
        )

    def pass_on(x, k, hi):
        if k == REACH - 1 and hi == 0:
            return
        copy = forward(x, k, hi)
        copy.start()
        sends.append(copy)

    def arrive(x, k, hi):
        forward(x, k - 1, hi).wait_recv()

    def relay(x, k):
        for hi in (1, 0):
            if k == REACH and hi == 0:
                continue
            if k == 0:
                gathered(x, hi)
            else:
                arrive(x, k, hi)
            if k < REACH:
                pass_on(x, k, hi)

    counts = []
    for t in range(2):
        block = 2 * seq + t
        gaps = [block - header[t]] + [block - related[t, r] for r in range(3)]
        row = []
        for d in range(SPAN):
            total = sum(
                (jnp.where(gap == d, 1.0, 0.0) for gap in gaps),
                1.0 if d < 2 else 0.0,
            )
            bias = jnp.where(total > 0.5, 0.0, -BIG)
            for n in range(2, SPAN):
                bias = jnp.where(total > n - 0.5, LOG2[n] / C2, bias)
            row.append(bias)
        counts.append(row)

    def pieces(k):
        if k == 0:
            return ((0, SPAN - 1, 1), (1, SPAN - 2, 2))
        if k == REACH:
            return ((0, 0, 1),)
        low = NPOS - 2 - 2 * k
        return ((0, low, 2), (1, low - 1, 2))

    def cols_of(n):
        return pl.ds(pl.multiple_of(n * QT, QT), QT)

    def scores(k):
        for t, row, blocks in pieces(k):
            keys = win.at[0, pl.ds((row + t) * BLOCK, blocks * BLOCK), :]
            bias = [counts[t][SPAN - 1 - row - b] for b in range(blocks)]

            def body(n, carry, t=t, row=row, blocks=blocks, keys=keys, bias=bias):
                cols = cols_of(n)
                q = q_r[pl.ds(pl.multiple_of(t * QROWS + n * QT, QT), QT), :]
                s = dot(keys[...], q, NT)
                tops = [
                    jnp.max(s[b * BLOCK : (b + 1) * BLOCK], axis=0, keepdims=True)
                    + jnp.minimum(bias[b], 0.0)
                    for b in range(blocks)
                ]
                top = functools.reduce(jnp.maximum, tops)
                if k > 0:
                    old = stats[t, 0:1, cols]
                    top = jnp.maximum(top, old)
                total = None
                for b in range(blocks):
                    shift = top - bias[b]
                    e = jnp.exp2((s[b * BLOCK : (b + 1) * BLOCK] - shift) * C2)
                    pbuf[t, pl.ds((row + b) * BLOCK, BLOCK), cols] = e
                    add = jnp.sum(e, axis=0, keepdims=True)
                    total = add if total is None else total + add
                if k > 0:
                    total = total + stats[t, 1:2, cols] * jnp.exp2((old - top) * C2)
                stats[t, 0:1, cols] = top
                stats[t, 1:2, cols] = total
                mhist[t, k : k + 1, cols] = top
                return carry

            lax.fori_loop(0, QROWS // QT, body, 0)

    def finish_sums():
        for t in range(2):
            inv = 1.0 / stats[t, 1:2, :]
            for k in range(REACH + 1 - t):
                mhist[t, k : k + 1, :] = (
                    jnp.exp2((mhist[t, k : k + 1, :] - stats[t, 0:1, :]) * C2) * inv
                )
            stats[t, 2:3, :] = jnp.zeros((1, QROWS), F32)

    def normalise(k):
        for t, row, blocks in pieces(k):
            rows = pl.ds(row * BLOCK, blocks * BLOCK)

            def body(n, carry, t=t, rows=rows):
                cols = cols_of(n)
                plow[t, rows, cols] = (
                    pbuf[t, rows, cols] * mhist[t, k : k + 1, cols]
                ).astype(BF16)
                return carry

            lax.fori_loop(0, QROWS // QT, body, 0)

    def dprobs(k):
        for t, row, blocks in pieces(k):
            rows = pl.ds(row * BLOCK, blocks * BLOCK)
            vals = win.at[1, pl.ds((row + t) * BLOCK, blocks * BLOCK), :]

            def body(n, carry, t=t, rows=rows, vals=vals):
                cols = cols_of(n)
                u = u_r[pl.ds(pl.multiple_of(t * QROWS + n * QT, QT), QT), :]
                dp = dot(vals[...], u, NT)
                dpbuf[t, rows, cols] = dp
                stats[t, 2:3, cols] += jnp.sum(
                    dp * plow[t, rows, cols].astype(F32), axis=0, keepdims=True
                )
                return carry

            lax.fori_loop(0, QROWS // QT, body, 0)

    def dscores(k):
        for t, row, blocks in pieces(k):
            rows = pl.ds(row * BLOCK, blocks * BLOCK)

            def body(n, carry, t=t, rows=rows):
                cols = cols_of(n)
                delta = stats[t, 2:3, cols]
                p = pbuf[t, rows, cols] * mhist[t, k : k + 1, cols]
                dlow[t, rows, cols] = (p * (dpbuf[t, rows, cols] - delta)).astype(BF16)
                return carry

            lax.fori_loop(0, QROWS // QT, body, 0)

    def terms(x, k):
        left, right, factor = (
            (dlow, q_r, SCALE),
            (plow, u_r, 1.0),
        )[x]
        found = {}
        for t, row, blocks in pieces(k):
            out = dot(
                left[t, pl.ds(row * BLOCK, blocks * BLOCK), :],
                right[pl.ds(t * QROWS, QROWS), :],
            )
            first = row + t - (NPOS - 2 - 2 * k)
            for b in range(blocks):
                hi = first + b
                term = out[b * BLOCK : (b + 1) * BLOCK]
                found[hi] = found[hi] + term if hi in found else term
        return {hi: term * factor for hi, term in found.items()}

    def backward(x, k, hi):
        return pltpu.make_async_remote_copy(
            src_ref=sbuf.at[x, k - 1, hi],
            dst_ref=rbuf.at[x, k - 1, hi],
            send_sem=r_send.at[x, k - 1, hi],
            recv_sem=r_recv.at[x, k - 1, hi],
            device_id={"seq": prv},
        )

    def local_terms(x, k):
        for hi, term in terms(x, k).items():
            widen[x, k, hi] = term

    def reduce_send(x, k):
        for hi in (1, 0):
            if k == REACH and hi == 0:
                continue
            total = widen[x, k, hi]
            if k < REACH - 1 or (k == REACH - 1 and hi == 1):
                backward(x, k + 1, hi).wait_recv()
                total = total + rbuf[x, k, hi].astype(F32)
            if k > 0:
                sbuf[x, k - 1, hi] = total.astype(BF16)
                copy = backward(x, k, hi)
                copy.start()
                sends.append(copy)
            else:
                gbuf[x, pl.ds(hi * BLOCK, BLOCK), :] = total.astype(BF16)

    def return_home(x):
        pltpu.make_async_copy(
            gbuf.at[x, pl.ds(me * part, part), :],
            backb.at[x, me],
            b_recv.at[x, me],
        ).start()
        for off in range(1, head_n):
            peer = lax.rem(me + off, head_n)
            copy = pltpu.make_async_remote_copy(
                src_ref=gbuf.at[x, pl.ds(peer * part, part), :],
                dst_ref=backb.at[x, me],
                send_sem=b_send.at[x, off],
                recv_sem=b_recv.at[x, me],
                device_id={"head": peer},
            )
            copy.start()
            sends.append(copy)

    outs = []

    def write_home(x, target):
        for h in range(head_n):
            ref = backb.at[x, h]
            pltpu.make_async_copy(ref, ref, b_recv.at[x, h]).wait()
            final[x, :, h * D : (h + 1) * D] = backb[x, h].astype(F32)
        copy = pltpu.make_async_copy(final.at[x], target, out_sem.at[x])
        copy.start()
        outs.append(copy)

    def transposes(x):
        for p in range(NPOS):
            at = pl.ds(p * BLOCK, BLOCK)
            tr[x, :, at] = win[x, at, :].T

    def row_output(x, left, stage, target, factor, slot):
        for t in range(2):

            def body(n, carry, t=t):
                cols = pl.ds(pl.multiple_of(n * 2 * D, 2 * D), 2 * D)
                out = dot(tr[x, :, pl.ds(t * BLOCK, SPAN * BLOCK)], left[t, :, cols])
                for s in range(2):
                    part_cols = pl.ds(pl.multiple_of((2 * n + s) * D, D), D)
                    stage[pl.ds(t * BLOCK, BLOCK), part_cols] = (
                        out[:, s * D : (s + 1) * D].T * factor
                    ).astype(BF16)
                return carry

            lax.fori_loop(0, GROUP // 2, body, 0)
        copy = pltpu.make_async_copy(stage, target, out_sem.at[slot])
        copy.start()
        outs.append(copy)

    relay(0, 0)
    for n in range(2 * GROUP):
        for copy in load(n):
            copy.wait()
    relay(1, 0)
    scores(0)
    for k in range(1, REACH):
        relay(0, k)
        relay(1, k)
        scores(k)
    relay(0, REACH)
    scores(REACH)
    finish_sums()
    normalise(REACH)
    local_terms(1, REACH)
    reduce_send(1, REACH)
    normalise(3)
    local_terms(1, 3)
    normalise(2)
    local_terms(1, 2)
    normalise(1)
    local_terms(1, 1)
    reduce_send(1, 3)
    normalise(0)
    local_terms(1, 0)
    dprobs(0)
    dprobs(1)
    reduce_send(1, 2)
    dprobs(2)
    dprobs(3)
    relay(1, REACH)
    dprobs(REACH)
    dscores(REACH)
    local_terms(0, REACH)
    reduce_send(0, REACH)
    reduce_send(1, 1)
    dscores(3)
    local_terms(0, 3)
    reduce_send(0, 3)
    dscores(2)
    local_terms(0, 2)
    reduce_send(1, 0)
    return_home(1)
    reduce_send(0, 2)
    dscores(1)
    local_terms(0, 1)
    reduce_send(0, 1)
    dscores(0)
    local_terms(0, 0)
    transposes(1)
    row_output(1, plow, att_v, att_hbm, 1.0, 2)
    reduce_send(0, 0)
    return_home(0)
    transposes(0)
    row_output(0, dlow, dq_v, dq_hbm, SCALE, 3)
    write_home(1, dv_hbm)
    write_home(0, dk_hbm)
    for copy in sends:
        copy.wait_send()
    for copy in outs:
        copy.wait()


def per_device(queries, keys, values, header, related, upstream):
    seq_n, head_n = lax.axis_size("seq"), lax.axis_size("head")
    part = keys.shape[0]
    any_space = pl.BlockSpec(memory_space=pl.ANY)
    scalars = pl.BlockSpec(memory_space=pltpu.SMEM)
    dma = pltpu.SemaphoreType.DMA
    return pl.pallas_call(
        functools.partial(kernel, seq_n, head_n),
        out_shape=(
            jax.ShapeDtypeStruct(queries.shape, BF16),
            jax.ShapeDtypeStruct(queries.shape, BF16),
            jax.ShapeDtypeStruct(keys.shape, F32),
            jax.ShapeDtypeStruct(values.shape, F32),
        ),
        in_specs=[scalars, scalars] + [any_space] * 4,
        out_specs=(any_space,) * 4,
        scratch_shapes=[
            pltpu.VMEM((2 * QROWS, D), BF16),
            pltpu.VMEM((2 * QROWS, D), BF16),
            pltpu.VMEM((2, NPOS * BLOCK, D), BF16),
            pltpu.VMEM((2, D, NPOS * BLOCK), BF16),
            pltpu.VMEM((2, SPAN * BLOCK, QROWS), F32),
            pltpu.VMEM((2, SPAN * BLOCK, QROWS), F32),
            pltpu.VMEM((2, SPAN * BLOCK, QROWS), BF16),
            pltpu.VMEM((2, SPAN * BLOCK, QROWS), BF16),
            pltpu.VMEM((2, 8, QROWS), F32),
            pltpu.VMEM((2, 8, QROWS), F32),
            pltpu.VMEM((2, REACH, 2, BLOCK, D), BF16),
            pltpu.VMEM((2, REACH, 2, BLOCK, D), BF16),
            pltpu.VMEM((2, 2 * BLOCK, D), BF16),
            pltpu.VMEM((2, head_n, part, D), BF16),
            pltpu.VMEM((2, REACH + 1, 2, BLOCK, D), F32),
            pltpu.VMEM((2, part, head_n * D), F32),
            pltpu.VMEM((2 * BLOCK, GROUP * D), BF16),
            pltpu.VMEM((2 * BLOCK, GROUP * D), BF16),
            dma((2, head_n)),
            dma((2, head_n)),
            dma((2, REACH, 2)),
            dma((2, REACH, 2)),
            dma((2, REACH, 2)),
            dma((2, REACH, 2)),
            dma((2, head_n)),
            dma((2, head_n)),
            dma((2, 2 * GROUP)),
            dma((4,)),
        ],
        compiler_params=pltpu.CompilerParams(
            collective_id=0,
            has_side_effects=True,
            vmem_limit_bytes=60 * 1024 * 1024,
        ),
        name="table_attention",
    )(header, related, queries, upstream, keys, values)


def solution(mesh):
    return jax.shard_map(
        per_device,
        mesh=mesh,
        in_specs=(
            P("seq", "head"),
            P(("seq", "head"), None),
            P(("seq", "head"), None),
            P("seq"),
            P("seq", None),
            P("seq", "head"),
        ),
        out_specs=(
            P("seq", "head"),
            P("seq", "head"),
            P(("seq", "head"), None),
            P(("seq", "head"), None),
        ),
        check_vma=False,
    )
```

```python
import functools
import math

import jax
import jax.numpy as jnp
from jax import lax
from jax.experimental import pallas as pl
from jax.experimental.pallas import tpu as pltpu
from jax.sharding import PartitionSpec as P

BLOCK = 128
D = 128
GROUP = 8
QROWS = BLOCK * GROUP
SPAN = 8
NPOS = 9
REACH = 4
QT = 512
BIG = 1e30
SCALE = 1.0 / math.sqrt(D)
C2 = SCALE * math.log2(math.e)
LOG2 = [math.log2(n) if n else 0.0 for n in range(SPAN)]
NT = (((1,), (1,)), ((), ()))
NN = (((1,), (0,)), ((), ()))
F32 = jnp.float32
BF16 = jnp.bfloat16


def dot(a, b, dims=NN):
    return lax.dot_general(a, b, dims, preferred_element_type=F32)


def kernel(
    seq_n,
    head_n,
    header_hbm,
    related_hbm,
    q_hbm,
    u_hbm,
    k_hbm,
    v_hbm,
    home,
    att_v,
    dq_v,
    q_r,
    u_r,
    win,
    tr,
    pbuf,
    dpbuf,
    plow,
    dlow,
    stats,
    mhist,
    dsum,
    sbuf,
    rbuf,
    gbuf,
    backb,
    widen,
    a_send,
    a_recv,
    f_send,
    f_recv,
    r_send,
    r_recv,
    b_send,
    b_recv,
    ld_sem,
    header,
    related,
    table_sem,
):
    seq = lax.axis_index("seq")
    me = lax.axis_index("head")
    nxt = lax.rem(seq + 1, seq_n)
    prv = lax.rem(seq + seq_n - 1, seq_n)
    part = (2 * BLOCK) // head_n
    half = head_n // 2
    own = (NPOS - 2) * BLOCK

    barrier = pltpu.get_barrier_semaphore()
    for off in range(1, head_n):
        pl.semaphore_signal(
            barrier, inc=1, device_id={"head": lax.rem(me + off, head_n)}
        )
    pl.semaphore_signal(barrier, inc=1, device_id={"seq": nxt})
    pl.semaphore_signal(barrier, inc=1, device_id={"seq": prv})

    def load(n):
        t, j = n // GROUP, n % GROUP
        rows, cols = pl.ds(t * BLOCK, BLOCK), pl.ds(j * D, D)
        at = pl.ds(n * BLOCK, BLOCK)
        return (
            pltpu.make_async_copy(q_hbm.at[rows, cols], q_r.at[at, :], ld_sem.at[0, n]),
            pltpu.make_async_copy(u_hbm.at[rows, cols], u_r.at[at, :], ld_sem.at[1, n]),
        )

    pl.semaphore_wait(barrier, head_n + 1)

    def mine(x, h):
        return pl.ds(own + h * part, part)

    sends = []
    for x, src in ((0, k_hbm), (1, v_hbm)):
        pltpu.make_async_copy(
            src.at[:, pl.ds(me * D, D)],
            win.at[x, pl.ds(own + me * part, part), :],
            a_recv.at[x, me],
        ).start()
        for off in range(1, head_n):
            peer = lax.rem(me + off, head_n)
            copy = pltpu.make_async_remote_copy(
                src_ref=src.at[:, pl.ds(peer * D, D)],
                dst_ref=win.at[x, pl.ds(own + me * part, part), :],
                send_sem=a_send.at[x, off],
                recv_sem=a_recv.at[x, me],
                device_id={"head": peer},
            )
            copy.start()
            sends.append(copy)

    tables = (
        pltpu.make_async_copy(header_hbm, header, table_sem.at[0]),
        pltpu.make_async_copy(related_hbm, related, table_sem.at[1]),
    )
    for copy in tables:
        copy.start()
    for n in range(2 * GROUP):
        for copy in load(n):
            copy.start()

    def gathered(x, hi):
        for h in range(half * hi, half * hi + half):
            ref = win.at[x, pl.ds(own + h * part, part), :]
            pltpu.make_async_copy(ref, ref, a_recv.at[x, h]).wait()

    def forward(x, k, hi):
        at = (NPOS - 2 - 2 * k + hi) * BLOCK
        return pltpu.make_async_remote_copy(
            src_ref=win.at[x, pl.ds(at, BLOCK), :],
            dst_ref=win.at[x, pl.ds(at - 2 * BLOCK, BLOCK), :],
            send_sem=f_send.at[x, k, hi],
            recv_sem=f_recv.at[x, k, hi],
            device_id={"seq": nxt},
        )

    def pass_on(x, k, hi):
        if k == REACH - 1 and hi == 0:
            return
        copy = forward(x, k, hi)
        copy.start()
        sends.append(copy)

    def arrive(x, k, hi):
        forward(x, k - 1, hi).wait_recv()

    def relay(x, k):
        for hi in (1, 0):
            if k == REACH and hi == 0:
                continue
            if k == 0:
                gathered(x, hi)
            else:
                arrive(x, k, hi)
            if k < REACH:
                pass_on(x, k, hi)

    def pieces(k):
        if k == 0:
            return ((0, SPAN - 1, 1), (1, SPAN - 2, 2))
        if k == REACH:
            return ((0, 0, 1),)
        low = NPOS - 2 - 2 * k
        return ((0, low, 2), (1, low - 1, 2))

    def cols_of(n):
        return pl.ds(pl.multiple_of(n * QT, QT), QT)

    def scores(k):
        for t, row, blocks in pieces(k):
            keys = win.at[0, pl.ds((row + t) * BLOCK, blocks * BLOCK), :]
            bias = [counts[t][SPAN - 1 - row - b] for b in range(blocks)]

            def body(n, carry, t=t, row=row, blocks=blocks, keys=keys, bias=bias):
                cols = cols_of(n)
                q = q_r[pl.ds(pl.multiple_of(t * QROWS + n * QT, QT), QT), :]
                s = dot(keys[...], q, NT)
                tops = [
                    jnp.max(s[b * BLOCK : (b + 1) * BLOCK], axis=0, keepdims=True)
                    + jnp.minimum(bias[b], 0.0)
                    for b in range(blocks)
                ]
                top = functools.reduce(jnp.maximum, tops)
                if k > 0:
                    old = stats[t, 0:1, cols]
                    top = jnp.maximum(top, old)
                total = None
                for b in range(blocks):
                    shift = top - bias[b]
                    e = jnp.exp2((s[b * BLOCK : (b + 1) * BLOCK] - shift) * C2)
                    pbuf[t, pl.ds((row + b) * BLOCK, BLOCK), cols] = e
                    add = jnp.sum(e, axis=0, keepdims=True)
                    total = add if total is None else total + add
                if k > 0:
                    total = total + stats[t, 1:2, cols] * jnp.exp2((old - top) * C2)
                stats[t, 0:1, cols] = top
                stats[t, 1:2, cols] = total
                mhist[t, k : k + 1, cols] = top
                return carry

            lax.fori_loop(0, QROWS // QT, body, 0)

    def finish_sums():
        for t in range(2):
            inv = 1.0 / stats[t, 1:2, :]
            for k in range(REACH + 1 - t):
                mhist[t, k : k + 1, :] = (
                    jnp.exp2((mhist[t, k : k + 1, :] - stats[t, 0:1, :]) * C2) * inv
                )

    def dprobs(k):
        for t, row, blocks in pieces(k):
            rows = pl.ds(row * BLOCK, blocks * BLOCK)
            vals = win.at[1, pl.ds((row + t) * BLOCK, blocks * BLOCK), :]

            def body(n, carry, t=t, rows=rows, vals=vals):
                cols = cols_of(n)
                u = u_r[pl.ds(pl.multiple_of(t * QROWS + n * QT, QT), QT), :]
                dp = dot(vals[...], u, NT)
                dpbuf[t, rows, cols] = dp
                dsum[t, k : k + 1, cols] = jnp.sum(
                    dp * pbuf[t, rows, cols], axis=0, keepdims=True
                )
                return carry

            lax.fori_loop(0, QROWS // QT, body, 0)

    def finish_delta():
        for t in range(2):
            stats[t, 2:3, :] = sum(
                mhist[t, k : k + 1, :] * dsum[t, k : k + 1, :]
                for k in range(REACH + 1 - t)
            )

    def settle(k, probs=True, grads=True):
        for t, row, blocks in pieces(k):
            rows = pl.ds(row * BLOCK, blocks * BLOCK)

            def body(n, carry, t=t, rows=rows):
                cols = cols_of(n)
                p = pbuf[t, rows, cols] * mhist[t, k : k + 1, cols]
                if probs:
                    plow[t, rows, cols] = p.astype(BF16)
                if grads:
                    delta = stats[t, 2:3, cols]
                    dlow[t, rows, cols] = (
                        p * (dpbuf[t, rows, cols] - delta)
                    ).astype(BF16)
                return carry

            lax.fori_loop(0, QROWS // QT, body, 0)

    def terms(x, k):
        left, right, factor = (
            (dlow, q_r, SCALE),
            (plow, u_r, 1.0),
        )[x]
        found = {}
        for t, row, blocks in pieces(k):
            out = dot(
                left[t, pl.ds(row * BLOCK, blocks * BLOCK), :],
                right[pl.ds(t * QROWS, QROWS), :],
            )
            first = row + t - (NPOS - 2 - 2 * k)
            for b in range(blocks):
                hi = first + b
                term = out[b * BLOCK : (b + 1) * BLOCK]
                found[hi] = found[hi] + term if hi in found else term
        return {hi: term * factor for hi, term in found.items()}

    def backward(x, k, hi):
        return pltpu.make_async_remote_copy(
            src_ref=sbuf.at[x, k - 1, hi],
            dst_ref=rbuf.at[x, k - 1, hi],
            send_sem=r_send.at[x, k - 1, hi],
            recv_sem=r_recv.at[x, k - 1, hi],
            device_id={"seq": prv},
        )

    def local_terms(x, k):
        for hi, term in terms(x, k).items():
            widen[x, k, hi] = term

    def reduce_send(x, k):
        for hi in (1, 0):
            if k == REACH and hi == 0:
                continue
            total = widen[x, k, hi]
            if k < REACH - 1 or (k == REACH - 1 and hi == 1):
                backward(x, k + 1, hi).wait_recv()
                total = total + rbuf[x, k, hi].astype(F32)
            if k > 0:
                sbuf[x, k - 1, hi] = total.astype(BF16)
                copy = backward(x, k, hi)
                copy.start()
                sends.append(copy)
            else:
                gbuf[x, pl.ds(hi * BLOCK, BLOCK), :] = total.astype(BF16)

    def return_home(x):
        pltpu.make_async_copy(
            gbuf.at[x, pl.ds(me * part, part), :],
            backb.at[x, me],
            b_recv.at[x, me],
        ).start()
        for off in range(1, head_n):
            peer = lax.rem(me + off, head_n)
            copy = pltpu.make_async_remote_copy(
                src_ref=gbuf.at[x, pl.ds(peer * part, part), :],
                dst_ref=backb.at[x, me],
                send_sem=b_send.at[x, off],
                recv_sem=b_recv.at[x, me],
                device_id={"head": peer},
            )
            copy.start()
            sends.append(copy)

    def write_home(x):
        for h in range(head_n):
            ref = backb.at[x, h]
            pltpu.make_async_copy(ref, ref, b_recv.at[x, h]).wait()
        home[x] = backb[x]

    def transposes(x):
        for p in range(NPOS):
            at = pl.ds(p * BLOCK, BLOCK)
            tr[x, :, at] = win[x, at, :].T

    def row_output(x, left, stage, factor):
        for t in range(2):

            def body(n, carry, t=t):
                cols = pl.ds(pl.multiple_of(n * 2 * D, 2 * D), 2 * D)
                out = dot(tr[x, :, pl.ds(t * BLOCK, SPAN * BLOCK)], left[t, :, cols])
                for s in range(2):
                    part_cols = pl.ds(pl.multiple_of((2 * n + s) * D, D), D)
                    stage[pl.ds(t * BLOCK, BLOCK), part_cols] = (
                        out[:, s * D : (s + 1) * D].T * factor
                    ).astype(BF16)
                return carry

            lax.fori_loop(0, GROUP // 2, body, 0)
    relay(0, 0)
    for copy in tables:
        copy.wait()
    counts = []
    for t in range(2):
        block = 2 * seq + t
        gaps = [block - header[t]] + [block - related[t, r] for r in range(3)]
        row = []
        for d in range(SPAN):
            total = sum(
                (jnp.where(gap == d, 1.0, 0.0) for gap in gaps),
                1.0 if d < 2 else 0.0,
            )
            bias = jnp.where(total > 0.5, 0.0, -BIG)
            for n in range(2, SPAN):
                bias = jnp.where(total > n - 0.5, LOG2[n] / C2, bias)
            row.append(bias)
        counts.append(row)

    for n in range(2 * GROUP):
        for copy in load(n):
            copy.wait()
    relay(1, 0)
    scores(0)
    dprobs(0)
    for k in range(1, REACH):
        relay(0, k)
        scores(k)
        relay(1, k)
        dprobs(k)
    relay(0, REACH)
    scores(REACH)
    finish_sums()
    settle(REACH, grads=False)
    local_terms(1, REACH)
    reduce_send(1, REACH)
    relay(1, REACH)
    dprobs(REACH)
    finish_delta()
    settle(REACH, probs=False)
    local_terms(0, REACH)
    reduce_send(0, REACH)
    settle(3)
    local_terms(1, 3)
    local_terms(0, 3)
    settle(2)
    reduce_send(1, 3)
    reduce_send(0, 3)
    local_terms(1, 2)
    local_terms(0, 2)
    settle(1)
    local_terms(1, 1)
    reduce_send(1, 2)
    reduce_send(0, 2)
    local_terms(0, 1)
    settle(0)
    local_terms(1, 0)
    local_terms(0, 0)
    reduce_send(1, 1)
    reduce_send(0, 1)
    transposes(1)
    row_output(1, plow, att_v, 1.0)
    transposes(0)
    reduce_send(1, 0)
    return_home(1)
    reduce_send(0, 0)
    return_home(0)
    row_output(0, dlow, dq_v, SCALE)
    write_home(1)
    write_home(0)
    for copy in sends:
        copy.wait_send()


def emit(home, att_v, dq_v, att, dq, dk, dv, wide, sems):
    copies = [
        pltpu.make_async_copy(att_v, att, sems.at[2]),
        pltpu.make_async_copy(dq_v, dq, sems.at[3]),
    ]
    for copy in copies:
        copy.start()
    for x, target in ((0, dk), (1, dv)):
        for h in range(home.shape[1]):
            wide[x, :, h * D : (h + 1) * D] = home[x, h].astype(F32)
        copy = pltpu.make_async_copy(wide.at[x], target, sems.at[x])
        copy.start()
        copies.append(copy)
    for copy in copies:
        copy.wait()


def per_device(queries, keys, values, header, related, upstream):
    seq_n, head_n = lax.axis_size("seq"), lax.axis_size("head")
    part = keys.shape[0]
    hbm = pl.BlockSpec(memory_space=pltpu.HBM)
    dma = pltpu.SemaphoreType.DMA
    vmem = pl.BlockSpec(memory_space=pltpu.VMEM)
    inputs = [
        pltpu.with_memory_space_constraint(x, pltpu.HBM)
        for x in (header, related, queries, upstream, keys, values)
    ]
    home, att, dq = pl.pallas_call(
        functools.partial(kernel, seq_n, head_n),
        out_shape=(
            jax.ShapeDtypeStruct((2, head_n, part, D), BF16),
            jax.ShapeDtypeStruct(queries.shape, BF16),
            jax.ShapeDtypeStruct(queries.shape, BF16),
        ),
        in_specs=[hbm] * 6,
        out_specs=(vmem,) * 3,
        scratch_shapes=[
            pltpu.VMEM((2 * QROWS, D), BF16),
            pltpu.VMEM((2 * QROWS, D), BF16),
            pltpu.VMEM((2, NPOS * BLOCK, D), BF16),
            pltpu.VMEM((2, D, NPOS * BLOCK), BF16),
            pltpu.VMEM((2, SPAN * BLOCK, QROWS), F32),
            pltpu.VMEM((2, SPAN * BLOCK, QROWS), F32),
            pltpu.VMEM((2, SPAN * BLOCK, QROWS), BF16),
            pltpu.VMEM((2, SPAN * BLOCK, QROWS), BF16),
            pltpu.VMEM((2, 8, QROWS), F32),
            pltpu.VMEM((2, 8, QROWS), F32),
            pltpu.VMEM((2, 8, QROWS), F32),
            pltpu.VMEM((2, REACH, 2, BLOCK, D), BF16),
            pltpu.VMEM((2, REACH, 2, BLOCK, D), BF16),
            pltpu.VMEM((2, 2 * BLOCK, D), BF16),
            pltpu.VMEM((2, head_n, part, D), BF16),
            pltpu.VMEM((2, REACH + 1, 2, BLOCK, D), F32),
            dma((2, head_n)),
            dma((2, head_n)),
            dma((2, REACH, 2)),
            dma((2, REACH, 2)),
            dma((2, REACH, 2)),
            dma((2, REACH, 2)),
            dma((2, head_n)),
            dma((2, head_n)),
            dma((2, 2 * GROUP)),
            pltpu.SMEM(header.shape, jnp.int32),
            pltpu.SMEM(related.shape, jnp.int32),
            dma((2,)),
        ],
        compiler_params=pltpu.CompilerParams(
            collective_id=0,
            has_side_effects=True,
            vmem_limit_bytes=44 * 1024 * 1024,
        ),
        name="table_attention",
    )(*inputs)
    return pl.pallas_call(
        emit,
        out_shape=(
            jax.ShapeDtypeStruct(queries.shape, BF16),
            jax.ShapeDtypeStruct(queries.shape, BF16),
            jax.ShapeDtypeStruct(keys.shape, F32),
            jax.ShapeDtypeStruct(values.shape, F32),
        ),
        in_specs=[vmem] * 3,
        out_specs=(hbm,) * 4,
        scratch_shapes=[pltpu.VMEM((2,) + keys.shape, F32), dma((4,))],
        compiler_params=pltpu.CompilerParams(vmem_limit_bytes=4 * 1024 * 1024),
        name="write_results",
    )(home, att, dq)


def solution(mesh):
    return jax.shard_map(
        per_device,
        mesh=mesh,
        in_specs=(
            P("seq", "head"),
            P(("seq", "head"), None),
            P(("seq", "head"), None),
            P("seq"),
            P("seq", None),
            P("seq", "head"),
        ),
        out_specs=(
            P("seq", "head"),
            P("seq", "head"),
            P(("seq", "head"), None),
            P(("seq", "head"), None),
        ),
        check_vma=False,
    )
```

```python
import functools
import math

import jax
import jax.numpy as jnp
from jax import lax
from jax.experimental import pallas as pl
from jax.experimental.pallas import tpu as pltpu
from jax.sharding import PartitionSpec as P

BLOCK = 128
D = 128
GROUP = 8
QROWS = BLOCK * GROUP
SPAN = 8
NPOS = 9
REACH = 4
QT = 512
BIG = 1e30
SCALE = 1.0 / math.sqrt(D)
C2 = SCALE * math.log2(math.e)
LOG2 = [math.log2(n) if n else 0.0 for n in range(SPAN)]
NT = (((1,), (1,)), ((), ()))
NN = (((1,), (0,)), ((), ()))
F32 = jnp.float32
BF16 = jnp.bfloat16


def dot(a, b, dims=NN):
    return lax.dot_general(a, b, dims, preferred_element_type=F32)


def kernel(
    seq_n,
    head_n,
    header_hbm,
    related_hbm,
    q_hbm,
    u_hbm,
    k_hbm,
    v_hbm,
    home,
    att_v,
    dq_v,
    q_r,
    u_r,
    win,
    tr,
    pbuf,
    dpbuf,
    plow,
    dlow,
    stats,
    mhist,
    dsum,
    sbuf,
    rbuf,
    gbuf,
    backb,
    backn,
    widen,
    a_send,
    a_recv,
    n_send,
    n_recv,
    f_send,
    f_recv,
    r_send,
    r_recv,
    b_send,
    b_recv,
    c_send,
    c_recv,
    ld_sem,
    header,
    related,
    table_sem,
):
    seq = lax.axis_index("seq")
    me = lax.axis_index("head")
    nxt = lax.rem(seq + 1, seq_n)
    prv = lax.rem(seq + seq_n - 1, seq_n)
    part = (2 * BLOCK) // head_n
    half = head_n // 2
    own = (NPOS - 2) * BLOCK

    barrier = pltpu.get_barrier_semaphore()
    for off in range(1, head_n):
        pl.semaphore_signal(
            barrier, inc=1, device_id={"head": lax.rem(me + off, head_n)}
        )
    for off in range(head_n):
        peer = lax.rem(me + off, head_n)
        for row in (nxt, prv):
            pl.semaphore_signal(barrier, inc=1, device_id={"seq": row, "head": peer})

    def load(n):
        t, j = n // GROUP, n % GROUP
        rows, cols = pl.ds(t * BLOCK, BLOCK), pl.ds(j * D, D)
        at = pl.ds(n * BLOCK, BLOCK)
        return (
            pltpu.make_async_copy(q_hbm.at[rows, cols], q_r.at[at, :], ld_sem.at[0, n]),
            pltpu.make_async_copy(u_hbm.at[rows, cols], u_r.at[at, :], ld_sem.at[1, n]),
        )

    pl.semaphore_wait(barrier, 3 * head_n - 1)

    sends = []
    ahead = own - 2 * BLOCK
    order = sorted(range(head_n), key=lambda off: -min(off, head_n - off))
    for x, src in ((0, k_hbm), (1, v_hbm)):
        pltpu.make_async_copy(
            src.at[:, pl.ds(me * D, D)],
            win.at[x, pl.ds(own + me * part, part), :],
            a_recv.at[x, me],
        ).start()
        for row, base, done, sent in (
            (nxt, ahead, n_recv, n_send),
            (seq, own, a_recv, a_send),
        ):
            for off in order:
                if row is seq and off == 0:
                    continue
                peer = lax.rem(me + off, head_n)
                copy = pltpu.make_async_remote_copy(
                    src_ref=src.at[:, pl.ds(peer * D, D)],
                    dst_ref=win.at[x, pl.ds(base + me * part, part), :],
                    send_sem=sent.at[x, off],
                    recv_sem=done.at[x, me],
                    device_id={"seq": row, "head": peer},
                )
                copy.start()
                sends.append(copy)

    tables = (
        pltpu.make_async_copy(header_hbm, header, table_sem.at[0]),
        pltpu.make_async_copy(related_hbm, related, table_sem.at[1]),
    )
    for copy in tables:
        copy.start()
    for n in range(2 * GROUP):
        for copy in load(n):
            copy.start()

    def gathered(x, hi, base, done):
        for h in range(half * hi, half * hi + half):
            ref = win.at[x, pl.ds(base + h * part, part), :]
            pltpu.make_async_copy(ref, ref, done.at[x, h]).wait()

    def own_rows(x):
        for hi in (1, 0):
            gathered(x, hi, own, a_recv)

    def forward(x, k, hi):
        at = (NPOS - 2 - 2 * k + hi) * BLOCK
        return pltpu.make_async_remote_copy(
            src_ref=win.at[x, pl.ds(at, BLOCK), :],
            dst_ref=win.at[x, pl.ds(at - 2 * BLOCK, BLOCK), :],
            send_sem=f_send.at[x, k - 1, hi],
            recv_sem=f_recv.at[x, k - 1, hi],
            device_id={"seq": nxt},
        )

    def relay(x, k, hi):
        if k == 1:
            gathered(x, hi, ahead, n_recv)
        else:
            forward(x, k - 1, hi).wait_recv()
        if k < REACH - 1 or (k == REACH - 1 and hi == 1):
            copy = forward(x, k, hi)
            copy.start()
            sends.append(copy)

    def pieces(k):
        if k == 0:
            return ((0, SPAN - 1, 1), (1, SPAN - 2, 2))
        if k == REACH:
            return ((0, 0, 1),)
        low = NPOS - 2 - 2 * k
        return ((0, low, 2), (1, low - 1, 2))

    def cols_of(n):
        return pl.ds(pl.multiple_of(n * QT, QT), QT)

    def scores(k, which=(0, 1)):
        for t, row, blocks in pieces(k):
            if t not in which:
                continue
            keys = win.at[0, pl.ds((row + t) * BLOCK, blocks * BLOCK), :]
            bias = [counts[t][SPAN - 1 - row - b] for b in range(blocks)]

            def body(n, carry, t=t, row=row, blocks=blocks, keys=keys, bias=bias):
                cols = cols_of(n)
                q = q_r[pl.ds(pl.multiple_of(t * QROWS + n * QT, QT), QT), :]
                s = dot(keys[...], q, NT)
                tops = [
                    jnp.max(s[b * BLOCK : (b + 1) * BLOCK], axis=0, keepdims=True)
                    + jnp.minimum(bias[b], 0.0)
                    for b in range(blocks)
                ]
                top = functools.reduce(jnp.maximum, tops)
                if k > 0:
                    old = stats[t, 0:1, cols]
                    top = jnp.maximum(top, old)
                total = None
                for b in range(blocks):
                    shift = top - bias[b]
                    e = jnp.exp2((s[b * BLOCK : (b + 1) * BLOCK] - shift) * C2)
                    pbuf[t, pl.ds((row + b) * BLOCK, BLOCK), cols] = e
                    add = jnp.sum(e, axis=0, keepdims=True)
                    total = add if total is None else total + add
                if k > 0:
                    total = total + stats[t, 1:2, cols] * jnp.exp2((old - top) * C2)
                stats[t, 0:1, cols] = top
                stats[t, 1:2, cols] = total
                mhist[t, k : k + 1, cols] = top
                return carry

            lax.fori_loop(0, QROWS // QT, body, 0)

    def finish_sums():
        for t in range(2):
            inv = 1.0 / stats[t, 1:2, :]
            for k in range(REACH + 1 - t):
                mhist[t, k : k + 1, :] = (
                    jnp.exp2((mhist[t, k : k + 1, :] - stats[t, 0:1, :]) * C2) * inv
                )

    def dprobs(k):
        for t, row, blocks in pieces(k):
            rows = pl.ds(row * BLOCK, blocks * BLOCK)
            vals = win.at[1, pl.ds((row + t) * BLOCK, blocks * BLOCK), :]

            def body(n, carry, t=t, rows=rows, vals=vals):
                cols = cols_of(n)
                u = u_r[pl.ds(pl.multiple_of(t * QROWS + n * QT, QT), QT), :]
                dp = dot(vals[...], u, NT)
                dpbuf[t, rows, cols] = dp
                dsum[t, k : k + 1, cols] = jnp.sum(
                    dp * pbuf[t, rows, cols], axis=0, keepdims=True
                )
                return carry

            lax.fori_loop(0, QROWS // QT, body, 0)

    def finish_delta():
        for t in range(2):
            stats[t, 2:3, :] = sum(
                mhist[t, k : k + 1, :] * dsum[t, k : k + 1, :]
                for k in range(REACH + 1 - t)
            )

    def settle(k, probs=True, grads=True):
        for t, row, blocks in pieces(k):
            rows = pl.ds(row * BLOCK, blocks * BLOCK)

            def body(n, carry, t=t, rows=rows):
                cols = cols_of(n)
                p = pbuf[t, rows, cols] * mhist[t, k : k + 1, cols]
                if probs:
                    plow[t, rows, cols] = p.astype(BF16)
                if grads:
                    delta = stats[t, 2:3, cols]
                    dlow[t, rows, cols] = (
                        p * (dpbuf[t, rows, cols] - delta)
                    ).astype(BF16)
                return carry

            lax.fori_loop(0, QROWS // QT, body, 0)

    def terms(x, k):
        left, right, factor = (
            (dlow, q_r, SCALE),
            (plow, u_r, 1.0),
        )[x]
        found = {}
        for t, row, blocks in pieces(k):
            out = dot(
                left[t, pl.ds(row * BLOCK, blocks * BLOCK), :],
                right[pl.ds(t * QROWS, QROWS), :],
            )
            first = row + t - (NPOS - 2 - 2 * k)
            for b in range(blocks):
                hi = first + b
                term = out[b * BLOCK : (b + 1) * BLOCK]
                found[hi] = found[hi] + term if hi in found else term
        return {hi: term * factor for hi, term in found.items()}

    def backward(x, k, hi):
        return pltpu.make_async_remote_copy(
            src_ref=sbuf.at[x, k - 1, hi],
            dst_ref=rbuf.at[x, k - 1, hi],
            send_sem=r_send.at[x, k - 1, hi],
            recv_sem=r_recv.at[x, k - 1, hi],
            device_id={"seq": prv},
        )

    def local_terms(x, k):
        for hi, term in terms(x, k).items():
            widen[x, k, hi] = term

    def reduce_send(x, k):
        for hi in (1, 0):
            if k == REACH and hi == 0:
                continue
            total = widen[x, k, hi]
            if k < REACH - 1 or (k == REACH - 1 and hi == 1):
                backward(x, k + 1, hi).wait_recv()
                total = total + rbuf[x, k, hi].astype(F32)
            sbuf[x, k - 1, hi] = total.astype(BF16)
            if k > 1:
                copy = backward(x, k, hi)
                copy.start()
                sends.append(copy)
                continue
            for h in range(half * hi, half * hi + half):
                at = h * part - hi * BLOCK
                copy = pltpu.make_async_remote_copy(
                    src_ref=sbuf.at[x, 0, hi, pl.ds(at, part), :],
                    dst_ref=backn.at[x, me],
                    send_sem=c_send.at[x, h],
                    recv_sem=c_recv.at[x, me],
                    device_id={"seq": prv, "head": h},
                )
                copy.start()
                sends.append(copy)

    def own_home(x):
        for hi in range(2):
            gbuf[x, pl.ds(hi * BLOCK, BLOCK), :] = widen[x, 0, hi].astype(BF16)
        pltpu.make_async_copy(
            gbuf.at[x, pl.ds(me * part, part), :],
            backb.at[x, me],
            b_recv.at[x, me],
        ).start()
        for off in range(1, head_n):
            peer = lax.rem(me + off, head_n)
            copy = pltpu.make_async_remote_copy(
                src_ref=gbuf.at[x, pl.ds(peer * part, part), :],
                dst_ref=backb.at[x, me],
                send_sem=b_send.at[x, off],
                recv_sem=b_recv.at[x, me],
                device_id={"head": peer},
            )
            copy.start()
            sends.append(copy)

    def write_home(x):
        for n, (buf, done) in enumerate(((backb, b_recv), (backn, c_recv))):
            for h in range(head_n):
                ref = buf.at[x, h]
                pltpu.make_async_copy(ref, ref, done.at[x, h]).wait()
            home[n, x] = buf[x]

    def transposes(x):
        for p in range(NPOS):
            at = pl.ds(p * BLOCK, BLOCK)
            tr[x, :, at] = win[x, at, :].T

    def row_output(x, left, stage, factor, which=(0, 1)):
        for t in which:

            def body(n, carry, t=t):
                cols = pl.ds(pl.multiple_of(n * 2 * D, 2 * D), 2 * D)
                out = dot(tr[x, :, pl.ds(t * BLOCK, SPAN * BLOCK)], left[t, :, cols])
                for s in range(2):
                    part_cols = pl.ds(pl.multiple_of((2 * n + s) * D, D), D)
                    stage[pl.ds(t * BLOCK, BLOCK), part_cols] = (
                        out[:, s * D : (s + 1) * D].T * factor
                    ).astype(BF16)
                return carry

            lax.fori_loop(0, GROUP // 2, body, 0)
    relay(0, 1, 1)
    relay(0, 1, 0)
    for copy in tables:
        copy.wait()
    counts = []
    for t in range(2):
        block = 2 * seq + t
        gaps = [block - header[t]] + [block - related[t, r] for r in range(3)]
        row = []
        for d in range(SPAN):
            total = sum(
                (jnp.where(gap == d, 1.0, 0.0) for gap in gaps),
                1.0 if d < 2 else 0.0,
            )
            bias = jnp.where(total > 0.5, 0.0, -BIG)
            for n in range(2, SPAN):
                bias = jnp.where(total > n - 0.5, LOG2[n] / C2, bias)
            row.append(bias)
        counts.append(row)

    for n in range(2 * GROUP):
        for copy in load(n):
            copy.wait()
    own_rows(0)
    relay(1, 1, 1)
    scores(0)
    relay(0, 2, 1)
    relay(0, 2, 0)
    relay(1, 1, 0)
    scores(1, (0,))
    relay(1, 2, 1)
    scores(1, (1,))
    relay(0, 3, 1)
    relay(0, 3, 0)
    relay(1, 2, 0)
    scores(2)
    relay(1, 3, 1)
    scores(3)
    relay(0, REACH, 1)
    scores(REACH)
    finish_sums()
    settle(REACH, grads=False)
    local_terms(1, REACH)
    reduce_send(1, REACH)
    own_rows(1)
    dprobs(0)
    dprobs(1)
    settle(3, grads=False)
    local_terms(1, 3)
    dprobs(2)
    relay(1, 3, 0)
    dprobs(3)
    relay(1, REACH, 1)
    dprobs(REACH)
    finish_delta()
    settle(REACH, probs=False)
    local_terms(0, REACH)
    reduce_send(0, REACH)
    reduce_send(1, 3)
    settle(3, probs=False)
    local_terms(0, 3)
    settle(2)
    local_terms(1, 2)
    reduce_send(0, 3)
    reduce_send(1, 2)
    local_terms(0, 2)
    settle(1)
    local_terms(1, 1)
    reduce_send(0, 2)
    reduce_send(1, 1)
    local_terms(0, 1)
    settle(0)
    reduce_send(0, 1)
    local_terms(1, 0)
    own_home(1)
    local_terms(0, 0)
    own_home(0)
    transposes(1)
    row_output(1, plow, att_v, 1.0)
    transposes(0)
    row_output(0, dlow, dq_v, SCALE)
    for copy in sends:
        copy.wait_send()
    write_home(1)
    write_home(0)


def emit(home, att_v, dq_v, att, dq, dk, dv, wide, sems):
    copies = [
        pltpu.make_async_copy(att_v, att, sems.at[2]),
        pltpu.make_async_copy(dq_v, dq, sems.at[3]),
    ]
    for copy in copies:
        copy.start()
    for x, target in ((0, dk), (1, dv)):
        for h in range(home.shape[2]):
            wide[x, :, h * D : (h + 1) * D] = home[0, x, h].astype(F32) + home[
                1, x, h
            ].astype(F32)
        copy = pltpu.make_async_copy(wide.at[x], target, sems.at[x])
        copy.start()
        copies.append(copy)
    for copy in copies:
        copy.wait()


def per_device(queries, keys, values, header, related, upstream):
    seq_n, head_n = lax.axis_size("seq"), lax.axis_size("head")
    part = keys.shape[0]
    hbm = pl.BlockSpec(memory_space=pltpu.HBM)
    dma = pltpu.SemaphoreType.DMA
    vmem = pl.BlockSpec(memory_space=pltpu.VMEM)
    inputs = [
        pltpu.with_memory_space_constraint(x, pltpu.HBM)
        for x in (header, related, queries, upstream, keys, values)
    ]
    home, att, dq = pl.pallas_call(
        functools.partial(kernel, seq_n, head_n),
        out_shape=(
            jax.ShapeDtypeStruct((2, 2, head_n, part, D), BF16),
            jax.ShapeDtypeStruct(queries.shape, BF16),
            jax.ShapeDtypeStruct(queries.shape, BF16),
        ),
        in_specs=[hbm] * 6,
        out_specs=(vmem,) * 3,
        scratch_shapes=[
            pltpu.VMEM((2 * QROWS, D), BF16),
            pltpu.VMEM((2 * QROWS, D), BF16),
            pltpu.VMEM((2, NPOS * BLOCK, D), BF16),
            pltpu.VMEM((2, D, NPOS * BLOCK), BF16),
            pltpu.VMEM((2, SPAN * BLOCK, QROWS), F32),
            pltpu.VMEM((2, SPAN * BLOCK, QROWS), F32),
            pltpu.VMEM((2, SPAN * BLOCK, QROWS), BF16),
            pltpu.VMEM((2, SPAN * BLOCK, QROWS), BF16),
            pltpu.VMEM((2, 8, QROWS), F32),
            pltpu.VMEM((2, 8, QROWS), F32),
            pltpu.VMEM((2, 8, QROWS), F32),
            pltpu.VMEM((2, REACH, 2, BLOCK, D), BF16),
            pltpu.VMEM((2, REACH, 2, BLOCK, D), BF16),
            pltpu.VMEM((2, 2 * BLOCK, D), BF16),
            pltpu.VMEM((2, head_n, part, D), BF16),
            pltpu.VMEM((2, head_n, part, D), BF16),
            pltpu.VMEM((2, REACH + 1, 2, BLOCK, D), F32),
            dma((2, head_n)),
            dma((2, head_n)),
            dma((2, head_n)),
            dma((2, head_n)),
            dma((2, REACH, 2)),
            dma((2, REACH, 2)),
            dma((2, REACH, 2)),
            dma((2, REACH, 2)),
            dma((2, head_n)),
            dma((2, head_n)),
            dma((2, head_n)),
            dma((2, head_n)),
            dma((2, 2 * GROUP)),
            pltpu.SMEM(header.shape, jnp.int32),
            pltpu.SMEM(related.shape, jnp.int32),
            dma((2,)),
        ],
        compiler_params=pltpu.CompilerParams(
            collective_id=0,
            has_side_effects=True,
            vmem_limit_bytes=44 * 1024 * 1024,
        ),
        name="table_attention",
    )(*inputs)
    return pl.pallas_call(
        emit,
        out_shape=(
            jax.ShapeDtypeStruct(queries.shape, BF16),
            jax.ShapeDtypeStruct(queries.shape, BF16),
            jax.ShapeDtypeStruct(keys.shape, F32),
            jax.ShapeDtypeStruct(values.shape, F32),
        ),
        in_specs=[vmem] * 3,
        out_specs=(hbm,) * 4,
        scratch_shapes=[pltpu.VMEM((2,) + keys.shape, F32), dma((4,))],
        compiler_params=pltpu.CompilerParams(vmem_limit_bytes=4 * 1024 * 1024),
        name="write_results",
    )(home, att, dq)


def solution(mesh):
    return jax.shard_map(
        per_device,
        mesh=mesh,
        in_specs=(
            P("seq", "head"),
            P(("seq", "head"), None),
            P(("seq", "head"), None),
            P("seq"),
            P("seq", None),
            P("seq", "head"),
        ),
        out_specs=(
            P("seq", "head"),
            P("seq", "head"),
            P(("seq", "head"), None),
            P(("seq", "head"), None),
        ),
        check_vma=False,
    )
```

```python
import functools
import math

import jax
import jax.numpy as jnp
from jax import lax
from jax.experimental import pallas as pl
from jax.experimental.pallas import tpu as pltpu
from jax.sharding import PartitionSpec as P

BLOCK = 128
D = 128
GROUP = 8
QROWS = BLOCK * GROUP
SPAN = 8
NPOS = 9
REACH = 4
QT = 512
CHUNK = 64
ORDER = (2, 3, 0, 1)
BIG = 1e30
SCALE = 1.0 / math.sqrt(D)
C2 = SCALE * math.log2(math.e)
LOG2 = [math.log2(n) if n else 0.0 for n in range(SPAN)]
NT = (((1,), (1,)), ((), ()))
NN = (((1,), (0,)), ((), ()))
F32 = jnp.float32
BF16 = jnp.bfloat16


def dot(a, b, dims=NN):
    return lax.dot_general(a, b, dims, preferred_element_type=F32)


def kernel(
    seq_n,
    head_n,
    header_hbm,
    related_hbm,
    q_hbm,
    u_hbm,
    k_hbm,
    v_hbm,
    home,
    att_v,
    dq_v,
    q_r,
    u_r,
    win,
    tr,
    pbuf,
    dpbuf,
    plow,
    dlow,
    stats,
    mhist,
    dsum,
    sbuf,
    rbuf,
    gbuf,
    backb,
    backn,
    widen,
    a_send,
    a_recv,
    n_send,
    n_recv,
    f_send,
    f_recv,
    r_send,
    r_recv,
    b_send,
    b_recv,
    c_send,
    c_recv,
    ld_sem,
    header,
    related,
    table_sem,
):
    seq = lax.axis_index("seq")
    me = lax.axis_index("head")
    nxt = lax.rem(seq + 1, seq_n)
    prv = lax.rem(seq + seq_n - 1, seq_n)
    part = (2 * BLOCK) // head_n
    quarter = head_n // 4
    own = (NPOS - 2) * BLOCK

    barrier = pltpu.get_barrier_semaphore()
    for off in range(1, head_n):
        pl.semaphore_signal(
            barrier, inc=1, device_id={"head": lax.rem(me + off, head_n)}
        )
    for off in range(head_n):
        peer = lax.rem(me + off, head_n)
        for row in (nxt, prv):
            pl.semaphore_signal(barrier, inc=1, device_id={"seq": row, "head": peer})

    def load(n):
        t, j = n // GROUP, n % GROUP
        rows, cols = pl.ds(t * BLOCK, BLOCK), pl.ds(j * D, D)
        at = pl.ds(n * BLOCK, BLOCK)
        return (
            pltpu.make_async_copy(q_hbm.at[rows, cols], q_r.at[at, :], ld_sem.at[0, n]),
            pltpu.make_async_copy(u_hbm.at[rows, cols], u_r.at[at, :], ld_sem.at[1, n]),
        )

    pl.semaphore_wait(barrier, 3 * head_n - 1)

    sends = []
    ahead = own - 2 * BLOCK
    order = sorted(range(head_n), key=lambda off: -min(off, head_n - off))
    for x, src in ((0, k_hbm), (1, v_hbm)):
        pltpu.make_async_copy(
            src.at[:, pl.ds(me * D, D)],
            win.at[x, pl.ds(own + me * part, part), :],
            a_recv.at[x, me],
        ).start()
        for row, base, done, sent in (
            (nxt, ahead, n_recv, n_send),
            (seq, own, a_recv, a_send),
        ):
            for off in order:
                if row is seq and off == 0:
                    continue
                peer = lax.rem(me + off, head_n)
                copy = pltpu.make_async_remote_copy(
                    src_ref=src.at[:, pl.ds(peer * D, D)],
                    dst_ref=win.at[x, pl.ds(base + me * part, part), :],
                    send_sem=sent.at[x, off],
                    recv_sem=done.at[x, me],
                    device_id={"seq": row, "head": peer},
                )
                copy.start()
                sends.append(copy)

    tables = (
        pltpu.make_async_copy(header_hbm, header, table_sem.at[0]),
        pltpu.make_async_copy(related_hbm, related, table_sem.at[1]),
    )
    for copy in tables:
        copy.start()
    for n in range(2 * GROUP):
        for copy in load(n):
            copy.start()

    def gathered(x, p, base, done):
        for h in range(p * quarter, p * quarter + quarter):
            ref = win.at[x, pl.ds(base + h * part, part), :]
            pltpu.make_async_copy(ref, ref, done.at[x, h]).wait()

    def own_rows(x):
        for p in ORDER:
            gathered(x, p, own, a_recv)

    def forward(x, k, p):
        at = (NPOS - 2 - 2 * k) * BLOCK + p * CHUNK
        return pltpu.make_async_remote_copy(
            src_ref=win.at[x, pl.ds(at, CHUNK), :],
            dst_ref=win.at[x, pl.ds(at - 2 * BLOCK, CHUNK), :],
            send_sem=f_send.at[x, k - 1, p],
            recv_sem=f_recv.at[x, k - 1, p],
            device_id={"seq": nxt},
        )

    def relay(x, k):
        for p in ORDER if k < REACH else ORDER[:2]:
            if k == 1:
                gathered(x, p, ahead, n_recv)
            else:
                forward(x, k - 1, p).wait_recv()
            if k < REACH - 1 or (k == REACH - 1 and p >= 2):
                copy = forward(x, k, p)
                copy.start()
                sends.append(copy)

    def pieces(k):
        if k == 0:
            return ((0, SPAN - 1, 1), (1, SPAN - 2, 2))
        if k == REACH:
            return ((0, 0, 1),)
        low = NPOS - 2 - 2 * k
        return ((0, low, 2), (1, low - 1, 2))

    def cols_of(n):
        return pl.ds(pl.multiple_of(n * QT, QT), QT)

    def scores(k, which=(0, 1)):
        for t, row, blocks in pieces(k):
            if t not in which:
                continue
            keys = win.at[0, pl.ds((row + t) * BLOCK, blocks * BLOCK), :]
            bias = [counts[t][SPAN - 1 - row - b] for b in range(blocks)]

            def body(n, carry, t=t, row=row, blocks=blocks, keys=keys, bias=bias):
                cols = cols_of(n)
                q = q_r[pl.ds(pl.multiple_of(t * QROWS + n * QT, QT), QT), :]
                s = dot(keys[...], q, NT)
                tops = [
                    jnp.max(s[b * BLOCK : (b + 1) * BLOCK], axis=0, keepdims=True)
                    + jnp.minimum(bias[b], 0.0)
                    for b in range(blocks)
                ]
                top = functools.reduce(jnp.maximum, tops)
                if k > 0:
                    old = stats[t, 0:1, cols]
                    top = jnp.maximum(top, old)
                total = None
                for b in range(blocks):
                    shift = top - bias[b]
                    e = jnp.exp2((s[b * BLOCK : (b + 1) * BLOCK] - shift) * C2)
                    pbuf[t, pl.ds((row + b) * BLOCK, BLOCK), cols] = e
                    add = jnp.sum(e, axis=0, keepdims=True)
                    total = add if total is None else total + add
                if k > 0:
                    total = total + stats[t, 1:2, cols] * jnp.exp2((old - top) * C2)
                stats[t, 0:1, cols] = top
                stats[t, 1:2, cols] = total
                mhist[t, k : k + 1, cols] = top
                return carry

            lax.fori_loop(0, QROWS // QT, body, 0)

    def finish_sums():
        for t in range(2):
            inv = 1.0 / stats[t, 1:2, :]
            for k in range(REACH + 1 - t):
                mhist[t, k : k + 1, :] = (
                    jnp.exp2((mhist[t, k : k + 1, :] - stats[t, 0:1, :]) * C2) * inv
                )

    def dprobs(k):
        for t, row, blocks in pieces(k):
            rows = pl.ds(row * BLOCK, blocks * BLOCK)
            vals = win.at[1, pl.ds((row + t) * BLOCK, blocks * BLOCK), :]

            def body(n, carry, t=t, rows=rows, vals=vals):
                cols = cols_of(n)
                u = u_r[pl.ds(pl.multiple_of(t * QROWS + n * QT, QT), QT), :]
                dp = dot(vals[...], u, NT)
                dpbuf[t, rows, cols] = dp
                dsum[t, k : k + 1, cols] = jnp.sum(
                    dp * pbuf[t, rows, cols], axis=0, keepdims=True
                )
                return carry

            lax.fori_loop(0, QROWS // QT, body, 0)

    def finish_delta():
        for t in range(2):
            stats[t, 2:3, :] = sum(
                mhist[t, k : k + 1, :] * dsum[t, k : k + 1, :]
                for k in range(REACH + 1 - t)
            )

    def settle(k, probs=True, grads=True):
        for t, row, blocks in pieces(k):
            rows = pl.ds(row * BLOCK, blocks * BLOCK)

            def body(n, carry, t=t, rows=rows):
                cols = cols_of(n)
                p = pbuf[t, rows, cols] * mhist[t, k : k + 1, cols]
                if probs:
                    plow[t, rows, cols] = p.astype(BF16)
                if grads:
                    delta = stats[t, 2:3, cols]
                    dlow[t, rows, cols] = (
                        p * (dpbuf[t, rows, cols] - delta)
                    ).astype(BF16)
                return carry

            lax.fori_loop(0, QROWS // QT, body, 0)

    def terms(x, k):
        left, right, factor = (
            (dlow, q_r, SCALE),
            (plow, u_r, 1.0),
        )[x]
        found = {}
        for t, row, blocks in pieces(k):
            out = dot(
                left[t, pl.ds(row * BLOCK, blocks * BLOCK), :],
                right[pl.ds(t * QROWS, QROWS), :],
            )
            first = row + t - (NPOS - 2 - 2 * k)
            for b in range(blocks):
                hi = first + b
                term = out[b * BLOCK : (b + 1) * BLOCK]
                found[hi] = found[hi] + term if hi in found else term
        return {hi: term * factor for hi, term in found.items()}

    def backward(x, k, p):
        rows = pl.ds(p * CHUNK, CHUNK)
        return pltpu.make_async_remote_copy(
            src_ref=sbuf.at[x, k - 1, rows, :],
            dst_ref=rbuf.at[x, k - 1, rows, :],
            send_sem=r_send.at[x, k - 1, p],
            recv_sem=r_recv.at[x, k - 1, p],
            device_id={"seq": prv},
        )

    def local_terms(x, k):
        for hi, term in terms(x, k).items():
            widen[x, k, pl.ds(hi * BLOCK, BLOCK), :] = term

    def reduce_send(x, k):
        for p in ORDER if k < REACH else ORDER[:2]:
            rows = pl.ds(p * CHUNK, CHUNK)
            total = widen[x, k, rows, :]
            if k < REACH - 1 or (k == REACH - 1 and p >= 2):
                backward(x, k + 1, p).wait_recv()
                total = total + rbuf[x, k, rows, :].astype(F32)
            sbuf[x, k - 1, rows, :] = total.astype(BF16)
            if k > 1:
                copy = backward(x, k, p)
                copy.start()
                sends.append(copy)
                continue
            for h in range(p * quarter, p * quarter + quarter):
                copy = pltpu.make_async_remote_copy(
                    src_ref=sbuf.at[x, 0, pl.ds(h * part, part), :],
                    dst_ref=backn.at[x, me],
                    send_sem=c_send.at[x, h],
                    recv_sem=c_recv.at[x, me],
                    device_id={"seq": prv, "head": h},
                )
                copy.start()
                sends.append(copy)

    def own_home(x):
        gbuf[x] = widen[x, 0].astype(BF16)
        pltpu.make_async_copy(
            gbuf.at[x, pl.ds(me * part, part), :],
            backb.at[x, me],
            b_recv.at[x, me],
        ).start()
        for off in range(1, head_n):
            peer = lax.rem(me + off, head_n)
            copy = pltpu.make_async_remote_copy(
                src_ref=gbuf.at[x, pl.ds(peer * part, part), :],
                dst_ref=backb.at[x, me],
                send_sem=b_send.at[x, off],
                recv_sem=b_recv.at[x, me],
                device_id={"head": peer},
            )
            copy.start()
            sends.append(copy)

    def write_home(x):
        for n, (buf, done) in enumerate(((backb, b_recv), (backn, c_recv))):
            for h in range(head_n):
                ref = buf.at[x, h]
                pltpu.make_async_copy(ref, ref, done.at[x, h]).wait()
            home[n, x] = buf[x]

    def transposes(x):
        for p in range(NPOS):
            at = pl.ds(p * BLOCK, BLOCK)
            tr[x, :, at] = win[x, at, :].T

    def row_output(x, left, stage, factor, which=(0, 1)):
        for t in which:

            def body(n, carry, t=t):
                cols = pl.ds(pl.multiple_of(n * 2 * D, 2 * D), 2 * D)
                out = dot(tr[x, :, pl.ds(t * BLOCK, SPAN * BLOCK)], left[t, :, cols])
                for s in range(2):
                    part_cols = pl.ds(pl.multiple_of((2 * n + s) * D, D), D)
                    stage[pl.ds(t * BLOCK, BLOCK), part_cols] = (
                        out[:, s * D : (s + 1) * D].T * factor
                    ).astype(BF16)
                return carry

            lax.fori_loop(0, GROUP // 2, body, 0)
    relay(0, 1)
    for copy in tables:
        copy.wait()
    counts = []
    for t in range(2):
        block = 2 * seq + t
        gaps = [block - header[t]] + [block - related[t, r] for r in range(3)]
        row = []
        for d in range(SPAN):
            total = sum(
                (jnp.where(gap == d, 1.0, 0.0) for gap in gaps),
                1.0 if d < 2 else 0.0,
            )
            bias = jnp.where(total > 0.5, 0.0, -BIG)
            for n in range(2, SPAN):
                bias = jnp.where(total > n - 0.5, LOG2[n] / C2, bias)
            row.append(bias)
        counts.append(row)

    for n in range(2 * GROUP):
        for copy in load(n):
            copy.wait()
    own_rows(0)
    scores(0)
    relay(1, 1)
    relay(0, 2)
    scores(1)
    own_rows(1)
    dprobs(0)
    relay(1, 2)
    relay(0, 3)
    scores(2)
    dprobs(1)
    relay(1, 3)
    scores(3)
    relay(0, REACH)
    scores(REACH)
    finish_sums()
    settle(REACH, grads=False)
    local_terms(1, REACH)
    reduce_send(1, REACH)
    dprobs(2)
    dprobs(3)
    relay(1, REACH)
    dprobs(REACH)
    finish_delta()
    settle(REACH, probs=False)
    local_terms(0, REACH)
    reduce_send(0, REACH)
    settle(3)
    local_terms(1, 3)
    reduce_send(1, 3)
    local_terms(0, 3)
    settle(2)
    local_terms(1, 2)
    reduce_send(0, 3)
    reduce_send(1, 2)
    local_terms(0, 2)
    settle(1)
    local_terms(1, 1)
    reduce_send(0, 2)
    reduce_send(1, 1)
    local_terms(0, 1)
    settle(0)
    local_terms(1, 0)
    own_home(1)
    local_terms(0, 0)
    own_home(0)
    reduce_send(0, 1)
    transposes(1)
    row_output(1, plow, att_v, 1.0)
    transposes(0)
    row_output(0, dlow, dq_v, SCALE)
    for copy in sends:
        copy.wait_send()
    write_home(1)
    write_home(0)


def emit(home, att_v, dq_v, att, dq, dk, dv, wide, sems):
    copies = [
        pltpu.make_async_copy(att_v, att, sems.at[2]),
        pltpu.make_async_copy(dq_v, dq, sems.at[3]),
    ]
    for copy in copies:
        copy.start()
    for x, target in ((0, dk), (1, dv)):
        for h in range(home.shape[2]):
            wide[x, :, h * D : (h + 1) * D] = home[0, x, h].astype(F32) + home[
                1, x, h
            ].astype(F32)
        copy = pltpu.make_async_copy(wide.at[x], target, sems.at[x])
        copy.start()
        copies.append(copy)
    for copy in copies:
        copy.wait()


def per_device(queries, keys, values, header, related, upstream):
    seq_n, head_n = lax.axis_size("seq"), lax.axis_size("head")
    part = keys.shape[0]
    hbm = pl.BlockSpec(memory_space=pltpu.HBM)
    dma = pltpu.SemaphoreType.DMA
    vmem = pl.BlockSpec(memory_space=pltpu.VMEM)
    inputs = [
        pltpu.with_memory_space_constraint(x, pltpu.HBM)
        for x in (header, related, queries, upstream, keys, values)
    ]
    home, att, dq = pl.pallas_call(
        functools.partial(kernel, seq_n, head_n),
        out_shape=(
            jax.ShapeDtypeStruct((2, 2, head_n, part, D), BF16),
            jax.ShapeDtypeStruct(queries.shape, BF16),
            jax.ShapeDtypeStruct(queries.shape, BF16),
        ),
        in_specs=[hbm] * 6,
        out_specs=(vmem,) * 3,
        scratch_shapes=[
            pltpu.VMEM((2 * QROWS, D), BF16),
            pltpu.VMEM((2 * QROWS, D), BF16),
            pltpu.VMEM((2, NPOS * BLOCK, D), BF16),
            pltpu.VMEM((2, D, NPOS * BLOCK), BF16),
            pltpu.VMEM((2, SPAN * BLOCK, QROWS), F32),
            pltpu.VMEM((2, SPAN * BLOCK, QROWS), F32),
            pltpu.VMEM((2, SPAN * BLOCK, QROWS), BF16),
            pltpu.VMEM((2, SPAN * BLOCK, QROWS), BF16),
            pltpu.VMEM((2, 8, QROWS), F32),
            pltpu.VMEM((2, 8, QROWS), F32),
            pltpu.VMEM((2, 8, QROWS), F32),
            pltpu.VMEM((2, REACH, 2 * BLOCK, D), BF16),
            pltpu.VMEM((2, REACH, 2 * BLOCK, D), BF16),
            pltpu.VMEM((2, 2 * BLOCK, D), BF16),
            pltpu.VMEM((2, head_n, part, D), BF16),
            pltpu.VMEM((2, head_n, part, D), BF16),
            pltpu.VMEM((2, REACH + 1, 2 * BLOCK, D), F32),
            dma((2, head_n)),
            dma((2, head_n)),
            dma((2, head_n)),
            dma((2, head_n)),
            dma((2, REACH, 4)),
            dma((2, REACH, 4)),
            dma((2, REACH, 4)),
            dma((2, REACH, 4)),
            dma((2, head_n)),
            dma((2, head_n)),
            dma((2, head_n)),
            dma((2, head_n)),
            dma((2, 2 * GROUP)),
            pltpu.SMEM(header.shape, jnp.int32),
            pltpu.SMEM(related.shape, jnp.int32),
            dma((2,)),
        ],
        compiler_params=pltpu.CompilerParams(
            collective_id=0,
            has_side_effects=True,
            vmem_limit_bytes=44 * 1024 * 1024,
        ),
        name="table_attention",
    )(*inputs)
    return pl.pallas_call(
        emit,
        out_shape=(
            jax.ShapeDtypeStruct(queries.shape, BF16),
            jax.ShapeDtypeStruct(queries.shape, BF16),
            jax.ShapeDtypeStruct(keys.shape, F32),
            jax.ShapeDtypeStruct(values.shape, F32),
        ),
        in_specs=[vmem] * 3,
        out_specs=(hbm,) * 4,
        scratch_shapes=[pltpu.VMEM((2,) + keys.shape, F32), dma((4,))],
        compiler_params=pltpu.CompilerParams(vmem_limit_bytes=4 * 1024 * 1024),
        name="write_results",
    )(home, att, dq)


def solution(mesh):
    return jax.shard_map(
        per_device,
        mesh=mesh,
        in_specs=(
            P("seq", "head"),
            P(("seq", "head"), None),
            P(("seq", "head"), None),
            P("seq"),
            P("seq", None),
            P("seq", "head"),
        ),
        out_specs=(
            P("seq", "head"),
            P("seq", "head"),
            P(("seq", "head"), None),
            P(("seq", "head"), None),
        ),
        check_vma=False,
    )
```

```python
import functools
import math

import jax
import jax.numpy as jnp
from jax import lax
from jax.experimental import pallas as pl
from jax.experimental.pallas import tpu as pltpu
from jax.sharding import PartitionSpec as P

BLOCK = 128
D = 128
GROUP = 8
QROWS = BLOCK * GROUP
SPAN = 8
NPOS = 9
REACH = 4
QT = 512
CHUNK = 64
ORDER = (2, 3, 0, 1)
BACK = (0, 1, 2, 3)
BIG = 1e30
SCALE = 1.0 / math.sqrt(D)
C2 = SCALE * math.log2(math.e)
LOG2 = [math.log2(n) if n else 0.0 for n in range(SPAN)]
NT = (((1,), (1,)), ((), ()))
NN = (((1,), (0,)), ((), ()))
F32 = jnp.float32
BF16 = jnp.bfloat16


def dot(a, b, dims=NN):
    return lax.dot_general(a, b, dims, preferred_element_type=F32)


def kernel(
    seq_n,
    head_n,
    header_hbm,
    related_hbm,
    q_hbm,
    u_hbm,
    k_hbm,
    v_hbm,
    home,
    att_v,
    dq_v,
    q_r,
    u_r,
    win,
    tr,
    pbuf,
    dpbuf,
    plow,
    dlow,
    stats,
    mhist,
    dsum,
    sbuf,
    rbuf,
    gbuf,
    backb,
    backn,
    widen,
    a_send,
    a_recv,
    n_send,
    n_recv,
    f_send,
    f_recv,
    r_send,
    r_recv,
    b_send,
    b_recv,
    c_send,
    c_recv,
    ld_sem,
    header,
    related,
    table_sem,
):
    seq = lax.axis_index("seq")
    me = lax.axis_index("head")
    nxt = lax.rem(seq + 1, seq_n)
    prv = lax.rem(seq + seq_n - 1, seq_n)
    part = (2 * BLOCK) // head_n
    quarter = head_n // 4
    own = (NPOS - 2) * BLOCK

    barrier = pltpu.get_barrier_semaphore()
    for off in range(1, head_n):
        pl.semaphore_signal(
            barrier, inc=1, device_id={"head": lax.rem(me + off, head_n)}
        )
    for off in range(head_n):
        peer = lax.rem(me + off, head_n)
        for row in (nxt, prv):
            pl.semaphore_signal(barrier, inc=1, device_id={"seq": row, "head": peer})

    def load(n):
        t, j = n // GROUP, n % GROUP
        rows, cols = pl.ds(t * BLOCK, BLOCK), pl.ds(j * D, D)
        at = pl.ds(n * BLOCK, BLOCK)
        return (
            pltpu.make_async_copy(q_hbm.at[rows, cols], q_r.at[at, :], ld_sem.at[0, n]),
            pltpu.make_async_copy(u_hbm.at[rows, cols], u_r.at[at, :], ld_sem.at[1, n]),
        )

    pl.semaphore_wait(barrier, 3 * head_n - 1)

    sends = []
    ahead = own - 2 * BLOCK
    order = sorted(range(head_n), key=lambda off: -min(off, head_n - off))
    for x, src in ((0, k_hbm), (1, v_hbm)):
        pltpu.make_async_copy(
            src.at[:, pl.ds(me * D, D)],
            win.at[x, pl.ds(own + me * part, part), :],
            a_recv.at[x, me],
        ).start()
        for row, base, done, sent in (
            (nxt, ahead, n_recv, n_send),
            (seq, own, a_recv, a_send),
        ):
            for off in order:
                if row is seq and off == 0:
                    continue
                peer = lax.rem(me + off, head_n)
                copy = pltpu.make_async_remote_copy(
                    src_ref=src.at[:, pl.ds(peer * D, D)],
                    dst_ref=win.at[x, pl.ds(base + me * part, part), :],
                    send_sem=sent.at[x, off],
                    recv_sem=done.at[x, me],
                    device_id={"seq": row, "head": peer},
                )
                copy.start()
                sends.append(copy)

    tables = (
        pltpu.make_async_copy(header_hbm, header, table_sem.at[0]),
        pltpu.make_async_copy(related_hbm, related, table_sem.at[1]),
    )
    for copy in tables:
        copy.start()
    for n in range(2 * GROUP):
        for copy in load(n):
            copy.start()

    def gathered(x, p, base, done):
        for h in range(p * quarter, p * quarter + quarter):
            ref = win.at[x, pl.ds(base + h * part, part), :]
            pltpu.make_async_copy(ref, ref, done.at[x, h]).wait()

    def own_rows(x):
        for p in ORDER:
            gathered(x, p, own, a_recv)

    def forward(x, k, p):
        at = (NPOS - 2 - 2 * k) * BLOCK + p * CHUNK
        return pltpu.make_async_remote_copy(
            src_ref=win.at[x, pl.ds(at, CHUNK), :],
            dst_ref=win.at[x, pl.ds(at - 2 * BLOCK, CHUNK), :],
            send_sem=f_send.at[x, k - 1, p],
            recv_sem=f_recv.at[x, k - 1, p],
            device_id={"seq": nxt},
        )

    def relay(x, k):
        for p in ORDER if k < REACH else ORDER[:2]:
            if k == 1:
                gathered(x, p, ahead, n_recv)
            else:
                forward(x, k - 1, p).wait_recv()
            if k < REACH - 1 or (k == REACH - 1 and p >= 2):
                copy = forward(x, k, p)
                copy.start()
                sends.append(copy)

    def pieces(k):
        if k == 0:
            return ((0, SPAN - 1, 1), (1, SPAN - 2, 2))
        if k == REACH:
            return ((0, 0, 1),)
        low = NPOS - 2 - 2 * k
        return ((0, low, 2), (1, low - 1, 2))

    def cols_of(n):
        return pl.ds(pl.multiple_of(n * QT, QT), QT)

    def scores(k, which=(0, 1)):
        for t, row, blocks in pieces(k):
            if t not in which:
                continue
            keys = win.at[0, pl.ds((row + t) * BLOCK, blocks * BLOCK), :]
            bias = [counts[t][SPAN - 1 - row - b] for b in range(blocks)]

            def body(n, carry, t=t, row=row, blocks=blocks, keys=keys, bias=bias):
                cols = cols_of(n)
                q = q_r[pl.ds(pl.multiple_of(t * QROWS + n * QT, QT), QT), :]
                s = dot(keys[...], q, NT)
                tops = [
                    jnp.max(s[b * BLOCK : (b + 1) * BLOCK], axis=0, keepdims=True)
                    + jnp.minimum(bias[b], 0.0)
                    for b in range(blocks)
                ]
                top = functools.reduce(jnp.maximum, tops)
                if k > 0:
                    old = stats[t, 0:1, cols]
                    top = jnp.maximum(top, old)
                total = None
                for b in range(blocks):
                    shift = top - bias[b]
                    e = jnp.exp2((s[b * BLOCK : (b + 1) * BLOCK] - shift) * C2)
                    pbuf[t, pl.ds((row + b) * BLOCK, BLOCK), cols] = e
                    add = jnp.sum(e, axis=0, keepdims=True)
                    total = add if total is None else total + add
                if k > 0:
                    total = total + stats[t, 1:2, cols] * jnp.exp2((old - top) * C2)
                stats[t, 0:1, cols] = top
                stats[t, 1:2, cols] = total
                mhist[t, k : k + 1, cols] = top
                return carry

            lax.fori_loop(0, QROWS // QT, body, 0, unroll=True)

    def finish_sums():
        for t in range(2):
            inv = 1.0 / stats[t, 1:2, :]
            for k in range(REACH + 1 - t):
                mhist[t, k : k + 1, :] = (
                    jnp.exp2((mhist[t, k : k + 1, :] - stats[t, 0:1, :]) * C2) * inv
                )

    def dprobs(k):
        for t, row, blocks in pieces(k):
            rows = pl.ds(row * BLOCK, blocks * BLOCK)
            vals = win.at[1, pl.ds((row + t) * BLOCK, blocks * BLOCK), :]

            def body(n, carry, t=t, rows=rows, vals=vals):
                cols = cols_of(n)
                u = u_r[pl.ds(pl.multiple_of(t * QROWS + n * QT, QT), QT), :]
                dp = dot(vals[...], u, NT)
                dpbuf[t, rows, cols] = dp
                dsum[t, k : k + 1, cols] = jnp.sum(
                    dp * pbuf[t, rows, cols], axis=0, keepdims=True
                )
                return carry

            lax.fori_loop(0, QROWS // QT, body, 0, unroll=True)

    def finish_delta():
        for t in range(2):
            stats[t, 2:3, :] = sum(
                mhist[t, k : k + 1, :] * dsum[t, k : k + 1, :]
                for k in range(REACH + 1 - t)
            )

    def settle(k, probs=True, grads=True):
        for t, row, blocks in pieces(k):
            rows = pl.ds(row * BLOCK, blocks * BLOCK)

            def body(n, carry, t=t, rows=rows):
                cols = cols_of(n)
                p = pbuf[t, rows, cols] * mhist[t, k : k + 1, cols]
                if probs:
                    plow[t, rows, cols] = p.astype(BF16)
                if grads:
                    delta = stats[t, 2:3, cols]
                    dlow[t, rows, cols] = (
                        p * (dpbuf[t, rows, cols] - delta)
                    ).astype(BF16)
                return carry

            lax.fori_loop(0, QROWS // QT, body, 0, unroll=True)

    def terms(x, k):
        left, right, factor = (
            (dlow, q_r, SCALE),
            (plow, u_r, 1.0),
        )[x]
        found = {}
        for t, row, blocks in pieces(k):
            out = dot(
                left[t, pl.ds(row * BLOCK, blocks * BLOCK), :],
                right[pl.ds(t * QROWS, QROWS), :],
            )
            first = row + t - (NPOS - 2 - 2 * k)
            for b in range(blocks):
                hi = first + b
                term = out[b * BLOCK : (b + 1) * BLOCK]
                found[hi] = found[hi] + term if hi in found else term
        return {hi: term * factor for hi, term in found.items()}

    def backward(x, k, p):
        rows = pl.ds(p * CHUNK, CHUNK)
        return pltpu.make_async_remote_copy(
            src_ref=sbuf.at[x, k - 1, rows, :],
            dst_ref=rbuf.at[x, k - 1, rows, :],
            send_sem=r_send.at[x, k - 1, p],
            recv_sem=r_recv.at[x, k - 1, p],
            device_id={"seq": prv},
        )

    def local_terms(x, k):
        for hi, term in terms(x, k).items():
            widen[x, k, pl.ds(hi * BLOCK, BLOCK), :] = term

    def reduce_send(x, k):
        for p in BACK if k < REACH else BACK[2:]:
            rows = pl.ds(p * CHUNK, CHUNK)
            total = widen[x, k, rows, :]
            if k < REACH - 1 or (k == REACH - 1 and p >= 2):
                backward(x, k + 1, p).wait_recv()
                total = total + rbuf[x, k, rows, :].astype(F32)
            sbuf[x, k - 1, rows, :] = total.astype(BF16)
            if k > 1:
                copy = backward(x, k, p)
                copy.start()
                sends.append(copy)
                continue
            for h in range(p * quarter, p * quarter + quarter):
                copy = pltpu.make_async_remote_copy(
                    src_ref=sbuf.at[x, 0, pl.ds(h * part, part), :],
                    dst_ref=backn.at[x, me],
                    send_sem=c_send.at[x, h],
                    recv_sem=c_recv.at[x, me],
                    device_id={"seq": prv, "head": h},
                )
                copy.start()
                sends.append(copy)

    def own_home(x):
        gbuf[x] = widen[x, 0].astype(BF16)
        pltpu.make_async_copy(
            gbuf.at[x, pl.ds(me * part, part), :],
            backb.at[x, me],
            b_recv.at[x, me],
        ).start()
        for off in range(1, head_n):
            peer = lax.rem(me + off, head_n)
            copy = pltpu.make_async_remote_copy(
                src_ref=gbuf.at[x, pl.ds(peer * part, part), :],
                dst_ref=backb.at[x, me],
                send_sem=b_send.at[x, off],
                recv_sem=b_recv.at[x, me],
                device_id={"head": peer},
            )
            copy.start()
            sends.append(copy)

    def write_home(x):
        for n, (buf, done) in enumerate(((backb, b_recv), (backn, c_recv))):
            for h in range(head_n):
                ref = buf.at[x, h]
                pltpu.make_async_copy(ref, ref, done.at[x, h]).wait()
            home[n, x] = buf[x]

    def transposes(x):
        for p in range(NPOS):
            at = pl.ds(p * BLOCK, BLOCK)
            tr[x, :, at] = win[x, at, :].T

    def row_output(x, left, stage, factor, which=(0, 1)):
        for t in which:

            def body(n, carry, t=t):
                cols = pl.ds(pl.multiple_of(n * 2 * D, 2 * D), 2 * D)
                out = dot(tr[x, :, pl.ds(t * BLOCK, SPAN * BLOCK)], left[t, :, cols])
                for s in range(2):
                    part_cols = pl.ds(pl.multiple_of((2 * n + s) * D, D), D)
                    stage[pl.ds(t * BLOCK, BLOCK), part_cols] = (
                        out[:, s * D : (s + 1) * D].T * factor
                    ).astype(BF16)
                return carry

            lax.fori_loop(0, GROUP // 2, body, 0)
    relay(0, 1)
    for copy in tables:
        copy.wait()
    counts = []
    for t in range(2):
        block = 2 * seq + t
        gaps = [block - header[t]] + [block - related[t, r] for r in range(3)]
        row = []
        for d in range(SPAN):
            total = sum(
                (jnp.where(gap == d, 1.0, 0.0) for gap in gaps),
                1.0 if d < 2 else 0.0,
            )
            bias = jnp.where(total > 0.5, 0.0, -BIG)
            for n in range(2, SPAN):
                bias = jnp.where(total > n - 0.5, LOG2[n] / C2, bias)
            row.append(bias)
        counts.append(row)

    for n in range(2 * GROUP):
        for copy in load(n):
            copy.wait()
    own_rows(0)
    scores(0)
    relay(1, 1)
    relay(0, 2)
    scores(1)
    own_rows(1)
    dprobs(0)
    relay(1, 2)
    relay(0, 3)
    scores(2)
    dprobs(1)
    relay(1, 3)
    scores(3)
    relay(0, REACH)
    scores(REACH)
    finish_sums()
    settle(REACH, grads=False)
    local_terms(1, REACH)
    reduce_send(1, REACH)
    dprobs(2)
    dprobs(3)
    relay(1, REACH)
    dprobs(REACH)
    finish_delta()
    settle(REACH, probs=False)
    local_terms(0, REACH)
    reduce_send(0, REACH)
    settle(3)
    local_terms(1, 3)
    reduce_send(1, 3)
    local_terms(0, 3)
    settle(2)
    local_terms(1, 2)
    reduce_send(0, 3)
    reduce_send(1, 2)
    local_terms(0, 2)
    settle(1)
    local_terms(1, 1)
    reduce_send(0, 2)
    reduce_send(1, 1)
    local_terms(0, 1)
    settle(0)
    local_terms(1, 0)
    own_home(1)
    local_terms(0, 0)
    own_home(0)
    reduce_send(0, 1)
    transposes(1)
    row_output(1, plow, att_v, 1.0)
    transposes(0)
    row_output(0, dlow, dq_v, SCALE)
    for copy in sends:
        copy.wait_send()
    write_home(1)
    write_home(0)


def emit(home, att_v, dq_v, att, dq, dk, dv, wide, sems):
    copies = [
        pltpu.make_async_copy(att_v, att, sems.at[2]),
        pltpu.make_async_copy(dq_v, dq, sems.at[3]),
    ]
    for copy in copies:
        copy.start()
    for x, target in ((0, dk), (1, dv)):
        for h in range(home.shape[2]):
            wide[x, :, h * D : (h + 1) * D] = home[0, x, h].astype(F32) + home[
                1, x, h
            ].astype(F32)
        copy = pltpu.make_async_copy(wide.at[x], target, sems.at[x])
        copy.start()
        copies.append(copy)
    for copy in copies:
        copy.wait()


def per_device(queries, keys, values, header, related, upstream):
    seq_n, head_n = lax.axis_size("seq"), lax.axis_size("head")
    part = keys.shape[0]
    hbm = pl.BlockSpec(memory_space=pltpu.HBM)
    dma = pltpu.SemaphoreType.DMA
    vmem = pl.BlockSpec(memory_space=pltpu.VMEM)
    inputs = [
        pltpu.with_memory_space_constraint(x, pltpu.HBM)
        for x in (header, related, queries, upstream, keys, values)
    ]
    home, att, dq = pl.pallas_call(
        functools.partial(kernel, seq_n, head_n),
        out_shape=(
            jax.ShapeDtypeStruct((2, 2, head_n, part, D), BF16),
            jax.ShapeDtypeStruct(queries.shape, BF16),
            jax.ShapeDtypeStruct(queries.shape, BF16),
        ),
        in_specs=[hbm] * 6,
        out_specs=(vmem,) * 3,
        scratch_shapes=[
            pltpu.VMEM((2 * QROWS, D), BF16),
            pltpu.VMEM((2 * QROWS, D), BF16),
            pltpu.VMEM((2, NPOS * BLOCK, D), BF16),
            pltpu.VMEM((2, D, NPOS * BLOCK), BF16),
            pltpu.VMEM((2, SPAN * BLOCK, QROWS), F32),
            pltpu.VMEM((2, SPAN * BLOCK, QROWS), F32),
            pltpu.VMEM((2, SPAN * BLOCK, QROWS), BF16),
            pltpu.VMEM((2, SPAN * BLOCK, QROWS), BF16),
            pltpu.VMEM((2, 8, QROWS), F32),
            pltpu.VMEM((2, 8, QROWS), F32),
            pltpu.VMEM((2, 8, QROWS), F32),
            pltpu.VMEM((2, REACH, 2 * BLOCK, D), BF16),
            pltpu.VMEM((2, REACH, 2 * BLOCK, D), BF16),
            pltpu.VMEM((2, 2 * BLOCK, D), BF16),
            pltpu.VMEM((2, head_n, part, D), BF16),
            pltpu.VMEM((2, head_n, part, D), BF16),
            pltpu.VMEM((2, REACH + 1, 2 * BLOCK, D), F32),
            dma((2, head_n)),
            dma((2, head_n)),
            dma((2, head_n)),
            dma((2, head_n)),
            dma((2, REACH, 4)),
            dma((2, REACH, 4)),
            dma((2, REACH, 4)),
            dma((2, REACH, 4)),
            dma((2, head_n)),
            dma((2, head_n)),
            dma((2, head_n)),
            dma((2, head_n)),
            dma((2, 2 * GROUP)),
            pltpu.SMEM(header.shape, jnp.int32),
            pltpu.SMEM(related.shape, jnp.int32),
            dma((2,)),
        ],
        compiler_params=pltpu.CompilerParams(
            collective_id=0,
            has_side_effects=True,
            vmem_limit_bytes=44 * 1024 * 1024,
        ),
        name="table_attention",
    )(*inputs)
    return pl.pallas_call(
        emit,
        out_shape=(
            jax.ShapeDtypeStruct(queries.shape, BF16),
            jax.ShapeDtypeStruct(queries.shape, BF16),
            jax.ShapeDtypeStruct(keys.shape, F32),
            jax.ShapeDtypeStruct(values.shape, F32),
        ),
        in_specs=[vmem] * 3,
        out_specs=(hbm,) * 4,
        scratch_shapes=[pltpu.VMEM((2,) + keys.shape, F32), dma((4,))],
        compiler_params=pltpu.CompilerParams(vmem_limit_bytes=4 * 1024 * 1024),
        name="write_results",
    )(home, att, dq)


def solution(mesh):
    return jax.shard_map(
        per_device,
        mesh=mesh,
        in_specs=(
            P("seq", "head"),
            P(("seq", "head"), None),
            P(("seq", "head"), None),
            P("seq"),
            P("seq", None),
            P("seq", "head"),
        ),
        out_specs=(
            P("seq", "head"),
            P("seq", "head"),
            P(("seq", "head"), None),
            P(("seq", "head"), None),
        ),
        check_vma=False,
    )
```

```python
import functools
import math

import jax
import jax.numpy as jnp
from jax import lax
from jax.experimental import pallas as pl
from jax.experimental.pallas import tpu as pltpu
from jax.sharding import PartitionSpec as P

BLOCK = 128
D = 128
GROUP = 8
QROWS = BLOCK * GROUP
SPAN = 8
NPOS = 9
REACH = 4
QT = 512
CHUNK = 64
ORDER = (2, 3, 0, 1)
BACK = (0, 1, 2, 3)
BIG = 1e30
SCALE = 1.0 / math.sqrt(D)
C2 = SCALE * math.log2(math.e)
LOG2 = [math.log2(n) if n else 0.0 for n in range(SPAN)]
NT = (((1,), (1,)), ((), ()))
NN = (((1,), (0,)), ((), ()))
F32 = jnp.float32
BF16 = jnp.bfloat16


def dot(a, b, dims=NN):
    return lax.dot_general(a, b, dims, preferred_element_type=F32)


def kernel(
    seq_n,
    head_n,
    header_hbm,
    related_hbm,
    q_hbm,
    u_hbm,
    k_hbm,
    v_hbm,
    home,
    att_v,
    dq_v,
    q_r,
    u_r,
    win,
    tr,
    pbuf,
    dpbuf,
    plow,
    dlow,
    stats,
    mhist,
    dsum,
    sbuf,
    rbuf,
    gbuf,
    backb,
    backn,
    widen,
    a_send,
    a_recv,
    n_send,
    n_recv,
    f_send,
    f_recv,
    r_send,
    r_recv,
    b_send,
    b_recv,
    c_send,
    c_recv,
    ld_sem,
    header,
    related,
    table_sem,
):
    seq = lax.axis_index("seq")
    me = lax.axis_index("head")
    nxt = lax.rem(seq + 1, seq_n)
    prv = lax.rem(seq + seq_n - 1, seq_n)
    part = (2 * BLOCK) // head_n
    quarter = head_n // 4
    own = (NPOS - 2) * BLOCK

    barrier = pltpu.get_barrier_semaphore()
    for off in range(1, head_n):
        pl.semaphore_signal(
            barrier, inc=1, device_id={"head": lax.rem(me + off, head_n)}
        )
    for off in range(head_n):
        peer = lax.rem(me + off, head_n)
        for row in (nxt, prv):
            pl.semaphore_signal(barrier, inc=1, device_id={"seq": row, "head": peer})

    def load(n):
        t, j = n // GROUP, n % GROUP
        rows, cols = pl.ds(t * BLOCK, BLOCK), pl.ds(j * D, D)
        at = pl.ds(n * BLOCK, BLOCK)
        return (
            pltpu.make_async_copy(q_hbm.at[rows, cols], q_r.at[at, :], ld_sem.at[0, n]),
            pltpu.make_async_copy(u_hbm.at[rows, cols], u_r.at[at, :], ld_sem.at[1, n]),
        )

    pl.semaphore_wait(barrier, 3 * head_n - 1)

    sends = []
    ahead = own - 2 * BLOCK
    order = sorted(range(head_n), key=lambda off: -min(off, head_n - off))
    for x, src in ((0, k_hbm), (1, v_hbm)):
        pltpu.make_async_copy(
            src.at[:, pl.ds(me * D, D)],
            win.at[x, pl.ds(own + me * part, part), :],
            a_recv.at[x, me],
        ).start()
        for row, base, done, sent in (
            (nxt, ahead, n_recv, n_send),
            (seq, own, a_recv, a_send),
        ):
            for off in order:
                if row is seq and off == 0:
                    continue
                peer = lax.rem(me + off, head_n)
                copy = pltpu.make_async_remote_copy(
                    src_ref=src.at[:, pl.ds(peer * D, D)],
                    dst_ref=win.at[x, pl.ds(base + me * part, part), :],
                    send_sem=sent.at[x, off],
                    recv_sem=done.at[x, me],
                    device_id={"seq": row, "head": peer},
                )
                copy.start()
                sends.append(copy)

    tables = (
        pltpu.make_async_copy(header_hbm, header, table_sem.at[0]),
        pltpu.make_async_copy(related_hbm, related, table_sem.at[1]),
    )
    for copy in tables:
        copy.start()
    for n in range(2 * GROUP):
        for copy in load(n):
            copy.start()

    def gathered(x, p, base, done):
        for h in range(p * quarter, p * quarter + quarter):
            ref = win.at[x, pl.ds(base + h * part, part), :]
            pltpu.make_async_copy(ref, ref, done.at[x, h]).wait()

    def own_rows(x):
        for p in ORDER:
            gathered(x, p, own, a_recv)

    def forward(x, k, p):
        at = (NPOS - 2 - 2 * k) * BLOCK + p * CHUNK
        return pltpu.make_async_remote_copy(
            src_ref=win.at[x, pl.ds(at, CHUNK), :],
            dst_ref=win.at[x, pl.ds(at - 2 * BLOCK, CHUNK), :],
            send_sem=f_send.at[x, k - 1, p],
            recv_sem=f_recv.at[x, k - 1, p],
            device_id={"seq": nxt},
        )

    def relay(x, k):
        for p in ORDER if k < REACH else ORDER[:2]:
            if k == 1:
                gathered(x, p, ahead, n_recv)
            else:
                forward(x, k - 1, p).wait_recv()
            if k < REACH - 1 or (k == REACH - 1 and p >= 2):
                copy = forward(x, k, p)
                copy.start()
                sends.append(copy)

    def pieces(k):
        if k == 0:
            return ((0, SPAN - 1, 1), (1, SPAN - 2, 2))
        if k == REACH:
            return ((0, 0, 1),)
        low = NPOS - 2 - 2 * k
        return ((0, low, 2), (1, low - 1, 2))

    def cols_of(n):
        return pl.ds(pl.multiple_of(n * QT, QT), QT)

    def scores(k, which=(0, 1)):
        for t, row, blocks in pieces(k):
            if t not in which:
                continue
            keys = win.at[0, pl.ds((row + t) * BLOCK, blocks * BLOCK), :]
            bias = [counts[t][SPAN - 1 - row - b] for b in range(blocks)]

            def body(n, carry, t=t, row=row, blocks=blocks, keys=keys, bias=bias):
                cols = cols_of(n)
                q = q_r[pl.ds(pl.multiple_of(t * QROWS + n * QT, QT), QT), :]
                s = dot(keys[...], q, NT)
                tops = [
                    jnp.max(s[b * BLOCK : (b + 1) * BLOCK], axis=0, keepdims=True)
                    + jnp.minimum(bias[b], 0.0)
                    for b in range(blocks)
                ]
                top = functools.reduce(jnp.maximum, tops)
                if k > 0:
                    old = stats[t, 0:1, cols]
                    top = jnp.maximum(top, old)
                total = None
                for b in range(blocks):
                    shift = top - bias[b]
                    e = jnp.exp2((s[b * BLOCK : (b + 1) * BLOCK] - shift) * C2)
                    pbuf[t, pl.ds((row + b) * BLOCK, BLOCK), cols] = e
                    add = jnp.sum(e, axis=0, keepdims=True)
                    total = add if total is None else total + add
                if k > 0:
                    total = total + stats[t, 1:2, cols] * jnp.exp2((old - top) * C2)
                stats[t, 0:1, cols] = top
                stats[t, 1:2, cols] = total
                mhist[t, k : k + 1, cols] = top
                return carry

            lax.fori_loop(0, QROWS // QT, body, 0, unroll=True)

    def finish_sums():
        for t in range(2):
            inv = 1.0 / stats[t, 1:2, :]
            for k in range(REACH + 1 - t):
                mhist[t, k : k + 1, :] = (
                    jnp.exp2((mhist[t, k : k + 1, :] - stats[t, 0:1, :]) * C2) * inv
                )

    def dprobs(k):
        for t, row, blocks in pieces(k):
            rows = pl.ds(row * BLOCK, blocks * BLOCK)
            vals = win.at[1, pl.ds((row + t) * BLOCK, blocks * BLOCK), :]

            def body(n, carry, t=t, rows=rows, vals=vals):
                cols = cols_of(n)
                u = u_r[pl.ds(pl.multiple_of(t * QROWS + n * QT, QT), QT), :]
                dp = dot(vals[...], u, NT)
                dpbuf[t, rows, cols] = dp
                dsum[t, k : k + 1, cols] = jnp.sum(
                    dp * pbuf[t, rows, cols], axis=0, keepdims=True
                )
                return carry

            lax.fori_loop(0, QROWS // QT, body, 0, unroll=True)

    def finish_delta():
        for t in range(2):
            stats[t, 2:3, :] = sum(
                mhist[t, k : k + 1, :] * dsum[t, k : k + 1, :]
                for k in range(REACH + 1 - t)
            )

    def settle(k, probs=True, grads=True):
        for t, row, blocks in pieces(k):
            rows = pl.ds(row * BLOCK, blocks * BLOCK)

            def body(n, carry, t=t, rows=rows):
                cols = cols_of(n)
                p = pbuf[t, rows, cols] * mhist[t, k : k + 1, cols]
                if probs:
                    plow[t, rows, cols] = p.astype(BF16)
                if grads:
                    delta = stats[t, 2:3, cols]
                    dlow[t, rows, cols] = (
                        p * (dpbuf[t, rows, cols] - delta)
                    ).astype(BF16)
                return carry

            lax.fori_loop(0, QROWS // QT, body, 0, unroll=True)

    def terms(x, k):
        left, right, factor = (
            (dlow, q_r, SCALE),
            (plow, u_r, 1.0),
        )[x]
        found = {}
        for t, row, blocks in pieces(k):
            out = dot(
                left[t, pl.ds(row * BLOCK, blocks * BLOCK), :],
                right[pl.ds(t * QROWS, QROWS), :],
            )
            first = row + t - (NPOS - 2 - 2 * k)
            for b in range(blocks):
                hi = first + b
                term = out[b * BLOCK : (b + 1) * BLOCK]
                found[hi] = found[hi] + term if hi in found else term
        return {hi: term * factor for hi, term in found.items()}

    def backward(x, k, p):
        rows = pl.ds(p * CHUNK, CHUNK)
        return pltpu.make_async_remote_copy(
            src_ref=sbuf.at[x, k - 1, rows, :],
            dst_ref=rbuf.at[x, k - 1, rows, :],
            send_sem=r_send.at[x, k - 1, p],
            recv_sem=r_recv.at[x, k - 1, p],
            device_id={"seq": prv},
        )

    def local_terms(x, k):
        for hi, term in terms(x, k).items():
            widen[x, k, pl.ds(hi * BLOCK, BLOCK), :] = term

    def reduce_send(x, k):
        for p in BACK if k < REACH else BACK[2:]:
            rows = pl.ds(p * CHUNK, CHUNK)
            total = widen[x, k, rows, :]
            if k < REACH - 1 or (k == REACH - 1 and p >= 2):
                backward(x, k + 1, p).wait_recv()
                total = total + rbuf[x, k, rows, :].astype(F32)
            sbuf[x, k - 1, rows, :] = total.astype(BF16)
            if k > 1:
                copy = backward(x, k, p)
                copy.start()
                sends.append(copy)
                continue
            for h in range(p * quarter, p * quarter + quarter):
                copy = pltpu.make_async_remote_copy(
                    src_ref=sbuf.at[x, 0, pl.ds(h * part, part), :],
                    dst_ref=backn.at[x, me],
                    send_sem=c_send.at[x, h],
                    recv_sem=c_recv.at[x, me],
                    device_id={"seq": prv, "head": h},
                )
                copy.start()
                sends.append(copy)

    def own_home(x):
        gbuf[x] = widen[x, 0].astype(BF16)
        pltpu.make_async_copy(
            gbuf.at[x, pl.ds(me * part, part), :],
            backb.at[x, me],
            b_recv.at[x, me],
        ).start()
        for off in range(1, head_n):
            peer = lax.rem(me + off, head_n)
            copy = pltpu.make_async_remote_copy(
                src_ref=gbuf.at[x, pl.ds(peer * part, part), :],
                dst_ref=backb.at[x, me],
                send_sem=b_send.at[x, off],
                recv_sem=b_recv.at[x, me],
                device_id={"head": peer},
            )
            copy.start()
            sends.append(copy)

    def write_home(x):
        for n, (buf, done) in enumerate(((backb, b_recv), (backn, c_recv))):
            for h in range(head_n):
                ref = buf.at[x, h]
                pltpu.make_async_copy(ref, ref, done.at[x, h]).wait()
            home[n, x] = buf[x]

    def transposes(x):
        for p in range(NPOS):
            at = pl.ds(p * BLOCK, BLOCK)
            tr[x, :, at] = win[x, at, :].T

    def row_output(x, left, stage, factor, which=(0, 1)):
        for t in which:

            def body(n, carry, t=t):
                cols = pl.ds(pl.multiple_of(n * 2 * D, 2 * D), 2 * D)
                out = dot(tr[x, :, pl.ds(t * BLOCK, SPAN * BLOCK)], left[t, :, cols])
                for s in range(2):
                    part_cols = pl.ds(pl.multiple_of((2 * n + s) * D, D), D)
                    stage[pl.ds(t * BLOCK, BLOCK), part_cols] = (
                        out[:, s * D : (s + 1) * D].T * factor
                    ).astype(BF16)
                return carry

            lax.fori_loop(0, GROUP // 2, body, 0)
    relay(0, 1)
    for copy in tables:
        copy.wait()
    counts = []
    for t in range(2):
        block = 2 * seq + t
        gaps = [block - header[t]] + [block - related[t, r] for r in range(3)]
        row = []
        for d in range(SPAN):
            total = sum(
                (jnp.where(gap == d, 1.0, 0.0) for gap in gaps),
                1.0 if d < 2 else 0.0,
            )
            bias = jnp.where(total > 0.5, 0.0, -BIG)
            for n in range(2, SPAN):
                bias = jnp.where(total > n - 0.5, LOG2[n] / C2, bias)
            row.append(bias)
        counts.append(row)

    for n in range(2 * GROUP):
        for copy in load(n):
            copy.wait()
    own_rows(0)
    scores(0)
    relay(1, 1)
    relay(0, 2)
    scores(1)
    own_rows(1)
    dprobs(0)
    relay(1, 2)
    relay(0, 3)
    scores(2)
    dprobs(1)
    relay(1, 3)
    scores(3)
    relay(0, REACH)
    scores(REACH)
    finish_sums()
    settle(REACH, grads=False)
    local_terms(1, REACH)
    reduce_send(1, REACH)
    dprobs(2)
    dprobs(3)
    relay(1, REACH)
    early = sends[:]
    sends.clear()
    dprobs(REACH)
    finish_delta()
    settle(REACH, probs=False)
    local_terms(0, REACH)
    reduce_send(0, REACH)
    settle(3)
    local_terms(1, 3)
    reduce_send(1, 3)
    local_terms(0, 3)
    settle(2)
    local_terms(1, 2)
    reduce_send(0, 3)
    reduce_send(1, 2)
    local_terms(0, 2)
    settle(1)
    local_terms(1, 1)
    for copy in early:
        copy.wait_send()
    reduce_send(0, 2)
    reduce_send(1, 1)
    local_terms(0, 1)
    settle(0)
    local_terms(1, 0)
    own_home(1)
    local_terms(0, 0)
    own_home(0)
    reduce_send(0, 1)
    transposes(1)
    row_output(1, plow, att_v, 1.0)
    transposes(0)
    row_output(0, dlow, dq_v, SCALE)
    for copy in sends:
        copy.wait_send()
    write_home(1)
    write_home(0)


def emit(home, att_v, dq_v, att, dq, dk, dv, wide, sems):
    copies = [
        pltpu.make_async_copy(att_v, att, sems.at[2]),
        pltpu.make_async_copy(dq_v, dq, sems.at[3]),
    ]
    for copy in copies:
        copy.start()
    for x, target in ((0, dk), (1, dv)):
        for h in range(home.shape[2]):
            wide[x, :, h * D : (h + 1) * D] = home[0, x, h].astype(F32) + home[
                1, x, h
            ].astype(F32)
        copy = pltpu.make_async_copy(wide.at[x], target, sems.at[x])
        copy.start()
        copies.append(copy)
    for copy in copies:
        copy.wait()


def per_device(queries, keys, values, header, related, upstream):
    seq_n, head_n = lax.axis_size("seq"), lax.axis_size("head")
    part = keys.shape[0]
    hbm = pl.BlockSpec(memory_space=pltpu.HBM)
    dma = pltpu.SemaphoreType.DMA
    vmem = pl.BlockSpec(memory_space=pltpu.VMEM)
    inputs = [
        pltpu.with_memory_space_constraint(x, pltpu.HBM)
        for x in (header, related, queries, upstream, keys, values)
    ]
    home, att, dq = pl.pallas_call(
        functools.partial(kernel, seq_n, head_n),
        out_shape=(
            jax.ShapeDtypeStruct((2, 2, head_n, part, D), BF16),
            jax.ShapeDtypeStruct(queries.shape, BF16),
            jax.ShapeDtypeStruct(queries.shape, BF16),
        ),
        in_specs=[hbm] * 6,
        out_specs=(vmem,) * 3,
        scratch_shapes=[
            pltpu.VMEM((2 * QROWS, D), BF16),
            pltpu.VMEM((2 * QROWS, D), BF16),
            pltpu.VMEM((2, NPOS * BLOCK, D), BF16),
            pltpu.VMEM((2, D, NPOS * BLOCK), BF16),
            pltpu.VMEM((2, SPAN * BLOCK, QROWS), F32),
            pltpu.VMEM((2, SPAN * BLOCK, QROWS), F32),
            pltpu.VMEM((2, SPAN * BLOCK, QROWS), BF16),
            pltpu.VMEM((2, SPAN * BLOCK, QROWS), BF16),
            pltpu.VMEM((2, 8, QROWS), F32),
            pltpu.VMEM((2, 8, QROWS), F32),
            pltpu.VMEM((2, 8, QROWS), F32),
            pltpu.VMEM((2, REACH, 2 * BLOCK, D), BF16),
            pltpu.VMEM((2, REACH, 2 * BLOCK, D), BF16),
            pltpu.VMEM((2, 2 * BLOCK, D), BF16),
            pltpu.VMEM((2, head_n, part, D), BF16),
            pltpu.VMEM((2, head_n, part, D), BF16),
            pltpu.VMEM((2, REACH + 1, 2 * BLOCK, D), F32),
            dma((2, head_n)),
            dma((2, head_n)),
            dma((2, head_n)),
            dma((2, head_n)),
            dma((2, REACH, 4)),
            dma((2, REACH, 4)),
            dma((2, REACH, 4)),
            dma((2, REACH, 4)),
            dma((2, head_n)),
            dma((2, head_n)),
            dma((2, head_n)),
            dma((2, head_n)),
            dma((2, 2 * GROUP)),
            pltpu.SMEM(header.shape, jnp.int32),
            pltpu.SMEM(related.shape, jnp.int32),
            dma((2,)),
        ],
        compiler_params=pltpu.CompilerParams(
            collective_id=0,
            has_side_effects=True,
            vmem_limit_bytes=44 * 1024 * 1024,
        ),
        name="table_attention",
    )(*inputs)
    return pl.pallas_call(
        emit,
        out_shape=(
            jax.ShapeDtypeStruct(queries.shape, BF16),
            jax.ShapeDtypeStruct(queries.shape, BF16),
            jax.ShapeDtypeStruct(keys.shape, F32),
            jax.ShapeDtypeStruct(values.shape, F32),
        ),
        in_specs=[vmem] * 3,
        out_specs=(hbm,) * 4,
        scratch_shapes=[pltpu.VMEM((2,) + keys.shape, F32), dma((4,))],
        compiler_params=pltpu.CompilerParams(vmem_limit_bytes=4 * 1024 * 1024),
        name="write_results",
    )(home, att, dq)


def solution(mesh):
    return jax.shard_map(
        per_device,
        mesh=mesh,
        in_specs=(
            P("seq", "head"),
            P(("seq", "head"), None),
            P(("seq", "head"), None),
            P("seq"),
            P("seq", None),
            P("seq", "head"),
        ),
        out_specs=(
            P("seq", "head"),
            P("seq", "head"),
            P(("seq", "head"), None),
            P(("seq", "head"), None),
        ),
        check_vma=False,
    )
```
